256 devices in a mesh: mp: 8 (over y, core), rows: 32 (over z, x).
Axes of the slice: x: 4, y: 4, z: 8, core: 2. Of those that a mesh axis runs over, the one named last changes fastest.
Arguments:
- hidden: bfloat16 [1024, 4096], P('rows'), may hold values from -60 to 60
- attn_gain: float32 [4096], replicated, may hold values from 0.3 to 1.7
- w_query: bfloat16 [4096, 4096], P(None, 'mp'), may hold values from -0.09375 to 0.09375
- w_key: bfloat16 [4096, 1024], P(None, 'mp'), may hold values from -0.09375 to 0.09375
- w_value: bfloat16 [4096, 1024], P(None, 'mp'), may hold values from -0.09375 to 0.09375
- w_output: bfloat16 [4096, 4096], P('mp'), may hold values from -0.09375 to 0.09375
- query_gain: float32 [128], replicated, may hold values from 0.5 to 1.5
- key_gain: float32 [128], replicated, may hold values from 0.5 to 1.5
- key_cache: bfloat16 [1024, 32, 1024], P('rows', None, 'mp'), may hold values from -730 to 730
- value_cache: bfloat16 [1024, 32, 1024], P('rows', None, 'mp'), may hold values from -6 to 6
- lengths: int32 [1024], P('rows'), may hold values from 1 to 32
- final_gain: float32 [4096], replicated, may hold values from 0.4 to 1.6
- old_embed: bfloat16 [1024, 4096], P('rows'), may hold values from -72 to 72
- slab: bfloat16 [16384, 4096], P('rows', 'mp'), may hold values from -6 to 6
- owners: int32 [16384, 1], P('rows'), may hold values from 0 to 31; in each aligned block of 512 rows (0 to 511, 512 to 1023, ...) at most 32 rows name the same one
Outputs:
- migrated: bfloat16 [32768, 4096], P('rows', 'mp')
The draws below stay inside these ranges and needn't reach their ends.
Inputs may be any that keep to these rules, and one draw needn't show every extreme that they name: `owners`: in each aligned block of 512 cache rows no owner is named by more than 32 rows.
All inputs are finite; a program needn't handle non-finite values.
Results may differ from the reference program's by a relative error of at most 0.008.
Values may be sent and summed in bfloat16 or wider, within the bound.
No kernel may reach another device: no remote copies, remote signals or barrier semaphores. Data moves between devices by JAX's collectives and lax.ppermute only.
A program may use at most 64 MiB of HBM per device.

```python
import math
import jax
import jax.numpy as jnp
import numpy as np
from jax import lax

D = 4096
HEADS = 32
KV_HEADS = 8
HEAD = 128
CTX = 32
ITERS = 3
CACHE_DEV = 512
ANCHORS = 1024
CACHE = 16384
CAP = 32
N_ROWS = 32


def draw_hidden(key, part):
    key_rows, key_cols, key_base = jax.random.split(key, 3)
    row_scale = jnp.exp(jax.random.uniform(key_rows, (ANCHORS, 1), minval=0.0, maxval=math.log(3.16)))
    col_scale = jnp.exp(jax.random.uniform(key_cols, (1, D), minval=0.0, maxval=math.log(3.16)))
    base = jnp.clip(jax.random.normal(key_base, (ANCHORS, D)), -6.0, 6.0)
    return (base * row_scale * col_scale).astype(jnp.bfloat16)


def draw_old_embed(key, part):
    key_rows, key_cols, key_base = jax.random.split(key, 3)
    row_scale = jnp.exp(jax.random.uniform(key_rows, (ANCHORS, 1), minval=0.0, maxval=math.log(2.0)))
    rising = 1.0 + 2.0 * jnp.arange(D, dtype=jnp.float32)[None, :] / D
    col_scale = rising * jnp.exp(jax.random.uniform(key_cols, (1, D), minval=0.0, maxval=math.log(2.0)))
    base = jnp.clip(jax.random.normal(key_base, (ANCHORS, D)), -6.0, 6.0)
    return (base * row_scale * col_scale).astype(jnp.bfloat16)


def draw_key_cache(key, part):
    key_base = jax.random.fold_in(key, 1)
    shape = (ANCHORS, CTX, KV_HEADS * HEAD)
    base = jnp.clip(jax.random.normal(key_base, shape), -6.0, 6.0)
    values = base
    return values.astype(jnp.bfloat16)


def touch_ends(drawn, rng, least, top_value):
    longest = drawn.shape.index(max(drawn.shape))
    spots = []
    for shift in (0, 1):
        where = [jax.random.randint(jax.random.fold_in(rng, axis), (), 0, length) for axis, length in enumerate(drawn.shape)]
        where[longest] = (where[longest] + shift) % drawn.shape[longest]
        spots.append(tuple(where))
    return drawn.at[spots[0]].set(least).at[spots[1]].set(top_value)


def level_of(rng, extent, cuts, least, high):
    def one(axis_at, blocks):
        draws = jax.random.uniform(jax.random.fold_in(jax.random.fold_in(rng, 6), axis_at), (blocks,), jnp.float32, least / len(cuts), high / len(cuts))
        return jnp.repeat(jnp.exp(draws), extent[axis_at] // blocks).reshape((-1,) + (1,) * (len(extent) - axis_at - 1))

    level = one(*cuts[0])
    for cut in cuts[1:]:
        level = level * one(*cut)
    return level


def deal_out(rng, own, number, rows, count, top, reach, lean):
    sequence = jax.random.permutation(rng, count)
    packed, usual = shares(count, rows * top, reach, lean, True), shares(count, rows * top, reach, lean, False)
    places = jnp.arange(count)

    def named(sizes, turn):
        used = int((sizes > 0).sum())
        fixed = max(1, used // 4)
        shifted = fixed + (places - fixed + turn * (used - fixed)) % max(1, count - fixed)
        return jnp.zeros((count,), jnp.int32).at[sequence[jnp.where(places < fixed, places, shifted)]].set(jnp.asarray(sizes, jnp.int32))

    sizes = jnp.where(number % 4 == 0, named(packed, number // 4), named(usual, number - number // 4 - 1))
    mixed = jax.random.permutation(jax.random.fold_in(own, 3), count)
    source_of, receiver = mixed[0:count // 2 * 2:2], mixed[1:count // 2 * 2:2]
    margin = jnp.minimum(sizes[source_of] - 1, reach - sizes[receiver]) // 2
    margin = jnp.where((source_of == sequence[0]) | (receiver == sequence[0]) | (sizes[receiver] == 0), 0, jnp.maximum(margin, 0))
    shifted = jax.random.randint(jax.random.fold_in(own, 4), (count // 2,), 0, 1 << 20) % (margin + 1)
    sizes = sizes.at[source_of].add(-shifted).at[receiver].add(shifted)
    labels = jnp.searchsorted(jnp.cumsum(sizes), jnp.arange(rows * top), side="right").astype(jnp.int32)
    table = labels.reshape(top, rows).T
    table = table[jax.random.permutation(jax.random.fold_in(own, 1), rows)]
    turn = jax.random.randint(jax.random.fold_in(own, 2), (rows, 1), 0, top)
    return jnp.take_along_axis(table, (jnp.arange(top)[None, :] + turn) % top, axis=1)


def shares(count, total, most, skew, full):
    weights = [(1 << 20) // math.isqrt(grade ** skew) + 1 for grade in range(1, count + 1)]
    largest = most if full else min(most, max(-(-total // count), total * weights[0] // sum(weights)))
    least = 1 if total - largest >= count - 1 else 0
    counts, spare = [largest] + [least] * (count - 1), total - largest - least * (count - 1)
    while spare > 0:
        movable = [i for i in range(1, count) if counts[i] < largest] or [i for i in range(1, count) if counts[i] < most]
        mass, remaining = sum([weights[i] for i in movable]), spare
        for i in movable:
            more = min(most - counts[i], max(1, remaining * weights[i] // mass), spare)
            counts[i] = counts[i] + more
            spare = spare - more
    return np.array(counts)


def bell_draw(stream_key, extent, spread, limit, shards=(), kind=jnp.bfloat16):
    drawn = spread * jax.random.normal(stream_key, extent, jnp.float32)
    if shards:
        drawn = drawn * level_of(stream_key, extent, shards, -0.22, 0.18)
    return jnp.clip(drawn, -limit, limit).astype(kind)


def setup_inputs(seed: int = 0) -> dict:
    keys = jax.random.split(jax.random.key(seed), 16)
    hidden = draw_hidden(jax.random.fold_in(keys[15], 71), 0)
    attn_gain = jnp.clip(jax.random.uniform(keys[1], (D,), jnp.float32, 0.3, 1.7), 0.3, 1.7)
    w_query = bell_draw(keys[2], (D, HEADS * HEAD), D ** -0.5, 0.09375, ((1, 8),))
    w_key = bell_draw(keys[3], (D, KV_HEADS * HEAD), D ** -0.5, 0.09375, ((1, 8),))
    w_value = bell_draw(keys[4], (D, KV_HEADS * HEAD), D ** -0.5, 0.09375, ((1, 8),))
    w_output = bell_draw(keys[5], (HEADS * HEAD, D), (HEADS * HEAD) ** -0.5, 0.09375, ((0, 8),))
    query_gain = jnp.clip(jax.random.uniform(keys[6], (HEAD,), jnp.float32, 0.5, 1.5), 0.5, 1.5)
    key_gain = jnp.clip(jax.random.uniform(keys[7], (HEAD,), jnp.float32, 0.5, 1.5), 0.5, 1.5)
    key_cache = draw_key_cache(jax.random.fold_in(keys[15], 71), 0)
    value_cache = bell_draw(keys[9], (ANCHORS, CTX, KV_HEADS * HEAD), 1.0, 6.0, ((0, 32), (2, 8)))
    lengths = touch_ends(jax.random.randint(keys[10], (ANCHORS,), 1, CTX + 1), jax.random.fold_in(keys[10], 1), 1, CTX).astype(jnp.int32)
    final_gain = jnp.clip(jax.random.uniform(keys[11], (D,), jnp.float32, 0.4, 1.6), 0.4, 1.6)
    old_embed = draw_old_embed(jax.random.fold_in(keys[15], 71), 0)
    slab = bell_draw(keys[13], (CACHE, D), 1.0, 6.0, ((0, 32), (1, 8)))
    owners_keys = jax.random.split(jax.random.fold_in(keys[14], 1), CACHE // CACHE_DEV)
    owners_turns = jax.random.permutation(jax.random.fold_in(keys[14], 3), CACHE // CACHE_DEV)
    owners = jax.vmap(lambda own, number: deal_out(jax.random.fold_in(keys[14], 2), own, number, CACHE_DEV, N_ROWS, 1, CAP, 2))(owners_keys, owners_turns).reshape((CACHE, 1))
    return {"hidden": hidden, "attn_gain": attn_gain, "w_query": w_query, "w_key": w_key, "w_value": w_value, "w_output": w_output, "query_gain": query_gain, "key_gain": key_gain, "key_cache": key_cache, "value_cache": value_cache, "lengths": lengths, "final_gain": final_gain, "old_embed": old_embed, "slab": slab, "owners": owners}


def rotate(values, position):
    half_width = values.shape[-1] // 2
    exponent = 2.0 * jnp.arange(half_width, dtype=jnp.float32) / values.shape[-1]
    frequency = jnp.exp(-exponent * math.log(1000000.0))
    angle = position[:, None, None] * frequency[None, None, :]
    cosine = jnp.cos(angle)
    sine = jnp.sin(angle)
    first = values[..., :half_width]
    second = values[..., half_width:]
    return jnp.concatenate([first * cosine - second * sine, second * cosine + first * sine], axis=-1)

def head_norm(values, gain):
    scale = lax.rsqrt(lax.optimization_barrier(jnp.mean(values * values, axis=-1, keepdims=True)) + 1e-06)
    return values * scale * gain

def reference(hidden, attn_gain, w_query, w_key, w_value, w_output, query_gain, key_gain, key_cache, value_cache, lengths, final_gain, old_embed, slab, owners):
    anchors = hidden.shape[0]
    group = HEADS // KV_HEADS
    hidden32 = hidden.astype(jnp.float32)
    normed = (hidden32 * lax.rsqrt(lax.optimization_barrier(jnp.mean(hidden32 * hidden32, axis=-1, keepdims=True)) + 1e-06) * attn_gain).astype(jnp.bfloat16)
    position = lengths.astype(jnp.float32)
    query = jnp.dot(normed, w_query, preferred_element_type=jnp.float32).reshape(anchors, HEADS, HEAD)
    query = rotate(head_norm(query, query_gain), position).astype(jnp.bfloat16)
    key_new = jnp.dot(normed, w_key, preferred_element_type=jnp.float32).reshape(anchors, KV_HEADS, HEAD)
    key_new = rotate(head_norm(key_new, key_gain), position).astype(jnp.bfloat16)
    value_new = jnp.dot(normed, w_value, preferred_element_type=jnp.float32).reshape(anchors, KV_HEADS, HEAD).astype(jnp.bfloat16)
    query32 = query.reshape(anchors, KV_HEADS, group, HEAD).astype(jnp.float32)
    keys32 = key_cache.reshape(anchors, CTX, KV_HEADS, HEAD).astype(jnp.float32)
    values32 = value_cache.reshape(anchors, CTX, KV_HEADS, HEAD).astype(jnp.float32)
    scale = 1.0 / math.sqrt(HEAD)
    scores = jnp.einsum('akgd,apkd->akgp', query32, keys32) * scale
    own_score = jnp.einsum('akgd,akd->akg', query32, key_new.astype(jnp.float32)) * scale
    valid = jnp.arange(CTX, dtype=jnp.int32)[None, :] < lengths[:, None]
    scores = jnp.where(valid[:, None, None, :], scores, -jnp.inf)
    top = jnp.maximum(lax.optimization_barrier(jnp.max(scores, axis=-1)), own_score)
    expo = jnp.exp(scores - top[..., None])
    own_expo = jnp.exp(own_score - top)
    total = lax.optimization_barrier(jnp.sum(expo, axis=-1)) + own_expo
    weights = (expo / total[..., None]).astype(jnp.bfloat16)
    own_weight = (own_expo / total).astype(jnp.bfloat16)
    attended = jnp.einsum('akgp,apkd->akgd', weights.astype(jnp.float32), values32)
    attended = attended + own_weight.astype(jnp.float32)[..., None] * value_new.astype(jnp.float32)[:, :, None, :]
    attended = attended.reshape(anchors, HEADS * HEAD).astype(jnp.bfloat16)
    state = hidden32 + jnp.dot(attended, w_output, preferred_element_type=jnp.float32)
    new_embed = (state * lax.rsqrt(lax.optimization_barrier(jnp.mean(state * state, axis=-1, keepdims=True)) + 1e-06) * final_gain).astype(jnp.bfloat16)
    cross = jnp.dot(old_embed.T, new_embed, preferred_element_type=jnp.float32)
    ridge = 0.125 * D
    highest = lax.Precision.HIGHEST
    old32 = old_embed.astype(jnp.float32)
    ridge_map = jnp.zeros_like(cross)
    residual = cross
    direction = cross
    res_sq = lax.optimization_barrier(jnp.sum(residual * residual, axis=0))
    for sweep in range(ITERS):
        image_docs = jnp.dot(old32, direction, precision=highest)
        curvature = lax.optimization_barrier(jnp.sum(image_docs * image_docs, axis=0)) + ridge * lax.optimization_barrier(jnp.sum(direction * direction, axis=0))
        alpha = res_sq / curvature
        ridge_map = ridge_map + alpha * direction
        image = jnp.dot(old32.T, image_docs, precision=highest) + ridge * direction
        residual = residual - alpha * image
        new_sq = lax.optimization_barrier(jnp.sum(residual * residual, axis=0))
        direction = residual + new_sq / res_sq * direction
        res_sq = new_sq
    map_b = ridge_map.astype(jnp.bfloat16)
    moved = jnp.dot(slab.astype(jnp.float32), map_b.astype(jnp.float32), preferred_element_type=jnp.float32).astype(jnp.bfloat16)
    owner_ids = owners[:, 0].reshape(N_ROWS, CACHE_DEV)
    onehot = (owner_ids[:, :, None] == jnp.arange(N_ROWS, dtype=jnp.int32)[None, None, :]).astype(jnp.int32)
    counted = jnp.cumsum(onehot, axis=1)
    slot = lax.optimization_barrier(jnp.sum((counted - 1) * onehot, axis=-1))
    source = jnp.arange(N_ROWS, dtype=jnp.int32)[:, None]
    target = ((owner_ids * N_ROWS + source) * CAP + slot).reshape(-1).astype(jnp.int32)
    migrated = jnp.zeros((N_ROWS * N_ROWS * CAP, D), jnp.bfloat16).at[target].set(moved)
    return migrated
```

```python
import math

import jax
import jax.numpy as jnp
from jax import lax
from jax.sharding import PartitionSpec as P

D = 4096
HEADS = 32
KV_HEADS = 8
HEAD = 128
ITERS = 3


def rotate(values, position):
    half_width = values.shape[-1] // 2
    exponent = 2.0 * jnp.arange(half_width, dtype=jnp.float32) / values.shape[-1]
    frequency = jnp.exp(-exponent * math.log(1000000.0))
    angle = position[:, None, None] * frequency[None, None, :]
    cosine = jnp.cos(angle)
    sine = jnp.sin(angle)
    first = values[..., :half_width]
    second = values[..., half_width:]
    return jnp.concatenate(
        [first * cosine - second * sine, second * cosine + first * sine], axis=-1
    )


def head_norm(values, gain):
    scale = lax.rsqrt(jnp.mean(values * values, axis=-1, keepdims=True) + 1e-06)
    return values * scale * gain


def contract_last(left, right):
    return lax.dot_general(
        left, right, (((1,), (1,)), ((), ())), preferred_element_type=jnp.float32
    )


def place(blocks, first):
    count = len(blocks)
    out = jnp.zeros((count,) + blocks[0].shape, blocks[0].dtype)
    for shift, block in enumerate(blocks):
        out = lax.dynamic_update_index_in_dim(out, block, (first + shift) % count, 0)
    return out


def ring(block, axis, count, size, stride):
    def move(array, step):
        pairs = []
        for i in range(size):
            at = i // stride % count
            pairs.append((i, i + ((at + step) % count - at) * stride))
        return lax.ppermute(array, axis, pairs)

    below, above = [block], [block]
    for _ in range(count // 2 - 1):
        below.append(move(below[-1], 1))
        above.append(move(above[-1], -1))
    half = block.shape[0] // 2
    far = jnp.concatenate([move(below[-1][:half], 1), move(above[-1][half:], -1)], axis=0)
    return above + [far] + below[:0:-1]


def gather_rows(block):
    size = lax.axis_size("rows")
    here = lax.axis_index("rows")
    line = 4
    row = place(ring(block, "rows", line, size, 1), here % line)
    row = row.reshape((line * block.shape[0],) + block.shape[1:])
    whole = place(ring(row, "rows", size // line, size, line), here // line)
    return whole.reshape((size * block.shape[0],) + block.shape[1:])


def gather_mp(block):
    size = lax.axis_size("mp")
    here = lax.axis_index("mp")
    own = jnp.stack(ring(block, "mp", size // 2, size, 2))
    other = lax.ppermute(own, "mp", [(i, i ^ 1) for i in range(size)])
    out = jnp.zeros((size,) + block.shape, block.dtype)
    for core, part in ((here % 2, own), (1 - here % 2, other)):
        for shift in range(size // 2):
            at = (here // 2 + shift) % (size // 2) * 2 + core
            out = lax.dynamic_update_index_in_dim(out, part[shift], at, 0)
    return out


def local(
    hidden,
    attn_gain,
    w_query,
    w_key,
    w_value,
    w_output,
    query_gain,
    key_gain,
    key_cache,
    value_cache,
    lengths,
    final_gain,
    old_embed,
    slab,
    owners,
):
    docs = hidden.shape[0]
    width = hidden.shape[1]
    kv_local = w_key.shape[1] // HEAD
    group = HEADS // KV_HEADS
    rows_count = lax.axis_size("rows")
    mp_count = lax.axis_size("mp")
    cols = width // mp_count
    highest = lax.Precision.HIGHEST
    hidden32 = hidden.astype(jnp.float32)
    normed = (
        hidden32
        * lax.rsqrt(jnp.mean(hidden32 * hidden32, axis=-1, keepdims=True) + 1e-06)
        * attn_gain
    ).astype(jnp.bfloat16)
    position = lengths.astype(jnp.float32)
    query = jnp.dot(normed, w_query, preferred_element_type=jnp.float32).reshape(
        docs, kv_local * group, HEAD
    )
    query = rotate(head_norm(query, query_gain), position).astype(jnp.bfloat16)
    key_new = jnp.dot(normed, w_key, preferred_element_type=jnp.float32).reshape(
        docs, kv_local, HEAD
    )
    key_new = rotate(head_norm(key_new, key_gain), position).astype(jnp.bfloat16)
    value_new = (
        jnp.dot(normed, w_value, preferred_element_type=jnp.float32)
        .reshape(docs, kv_local, HEAD)
        .astype(jnp.bfloat16)
    )
    query_groups = query.reshape(docs, kv_local, group, HEAD)
    keys = key_cache.reshape(docs, key_cache.shape[1], kv_local, HEAD)
    values = value_cache.reshape(docs, value_cache.shape[1], kv_local, HEAD)
    scale = 1.0 / math.sqrt(HEAD)
    scores = (
        jnp.einsum("akgd,apkd->akgp", query_groups, keys, preferred_element_type=jnp.float32)
        * scale
    )
    own_score = (
        jnp.einsum("akgd,akd->akg", query_groups, key_new, preferred_element_type=jnp.float32)
        * scale
    )
    valid = jnp.arange(keys.shape[1], dtype=jnp.int32)[None, :] < lengths[:, None]
    scores = jnp.where(valid[:, None, None, :], scores, -jnp.inf)
    top = jnp.maximum(jnp.max(scores, axis=-1), own_score)
    expo = jnp.exp(scores - top[..., None])
    own_expo = jnp.exp(own_score - top)
    total = jnp.sum(expo, axis=-1) + own_expo
    weights = (expo / total[..., None]).astype(jnp.bfloat16)
    own_weight = (own_expo / total).astype(jnp.bfloat16)
    attended = jnp.einsum("akgp,apkd->akgd", weights, values, preferred_element_type=jnp.float32)
    attended = (
        attended
        + own_weight.astype(jnp.float32)[..., None] * value_new.astype(jnp.float32)[:, :, None, :]
    )
    attended = attended.reshape(docs, kv_local * group * HEAD).astype(jnp.bfloat16)
    partial_value = jnp.dot(attended, w_output, preferred_element_type=jnp.float32)
    mine = lax.axis_index("mp") * cols
    my_cols = lambda array, axis: lax.dynamic_slice_in_dim(array, mine, cols, axis)
    pieces = partial_value.astype(jnp.bfloat16).reshape(docs, mp_count, cols).transpose(1, 0, 2)
    pieces = lax.all_to_all(pieces, "mp", 0, 0, tiled=True)
    state = my_cols(hidden32, 1) + jnp.sum(pieces.astype(jnp.float32), axis=0)
    squares = jnp.broadcast_to(jnp.sum(state * state, axis=-1)[None, :], (mp_count, docs))
    squares = jnp.sum(lax.all_to_all(squares, "mp", 0, 0, tiled=True), axis=0)
    new_embed = (
        state * lax.rsqrt(squares / width + 1e-06)[:, None] * my_cols(final_gain, 0)
    ).astype(jnp.bfloat16)

    old_mine = my_cols(old_embed, 1)
    old_all = gather_rows(old_mine)
    anchors = old_all.shape[0]
    part = anchors // mp_count
    slab_part = contract_last(slab, old_all).astype(jnp.bfloat16)
    slab_part = slab_part.reshape(-1, mp_count, part).transpose(1, 0, 2)
    slab_part = lax.all_to_all(slab_part, "mp", 0, 0, tiled=True)
    slab_dual = jnp.sum(slab_part.astype(jnp.float32), axis=0).astype(jnp.bfloat16)
    gram_part = contract_last(old_mine, old_all).reshape(docs, mp_count, part).transpose(1, 0, 2)
    gram_part = jnp.sum(lax.all_to_all(gram_part, "mp", 0, 0, tiled=True), axis=0)
    gram = gather_mp(gather_rows(gram_part).T).reshape(anchors, anchors)

    capacity = 2 * slab.shape[0] // rows_count
    owner_ids = owners[:, 0]
    onehot = (owner_ids[:, None] == jnp.arange(rows_count, dtype=jnp.int32)[None, :]).astype(
        jnp.int32
    )
    counted = jnp.cumsum(onehot, axis=0)
    slot = jnp.sum((counted - 1) * onehot, axis=-1)
    target = owner_ids * capacity + slot
    outgoing = jnp.zeros((rows_count * capacity, part), jnp.bfloat16).at[target].set(slab_dual)
    routed = lax.all_to_all(outgoing, "rows", split_axis=0, concat_axis=0, tiled=True)
    routed = gather_mp(routed)

    new_all = gather_rows(new_embed)
    ridge = 0.125 * D
    residual = new_all.astype(jnp.float32)
    image = jnp.dot(gram, residual, precision=highest)
    direction = residual
    direction_image = image
    dual_map = jnp.zeros_like(residual)
    res_sq = jnp.sum(residual * image, axis=0)
    for sweep in range(ITERS):
        curvature = jnp.sum(
            direction_image * (direction_image + ridge * direction), axis=0
        )
        alpha = res_sq / curvature
        dual_map = dual_map + alpha * direction
        if sweep + 1 < ITERS:
            residual = residual - alpha * (direction_image + ridge * direction)
            image = jnp.dot(gram, residual, precision=highest)
            new_sq = jnp.sum(residual * image, axis=0)
            direction = residual + new_sq / res_sq * direction
            direction_image = image + new_sq / res_sq * direction_image
            res_sq = new_sq
    dual_map = dual_map.astype(jnp.bfloat16).reshape(mp_count, part, cols)
    return lax.dot_general(
        routed,
        dual_map,
        (((0, 2), (0, 1)), ((), ())),
        preferred_element_type=jnp.float32,
    ).astype(jnp.bfloat16)


def solution(mesh):
    return jax.shard_map(
        local,
        mesh=mesh,
        in_specs=(
            P("rows", None),
            P(),
            P(None, "mp"),
            P(None, "mp"),
            P(None, "mp"),
            P("mp", None),
            P(),
            P(),
            P("rows", None, "mp"),
            P("rows", None, "mp"),
            P("rows"),
            P(),
            P("rows", None),
            P("rows", "mp"),
            P("rows", None),
        ),
        out_specs=P("rows", "mp"),
        check_vma=False,
    )
```

```python
import math

import jax
import jax.numpy as jnp
from jax import lax
from jax.experimental import pallas as pl
from jax.experimental.pallas import tpu as pltpu
from jax.sharding import PartitionSpec as P

D = 4096
HEADS = 32
KV_HEADS = 8
HEAD = 128
ITERS = 3


def rotate(values, position):
    half_width = values.shape[-1] // 2
    exponent = 2.0 * jnp.arange(half_width, dtype=jnp.float32) / values.shape[-1]
    frequency = jnp.exp(-exponent * math.log(1000000.0))
    angle = position[:, None, None] * frequency[None, None, :]
    cosine = jnp.cos(angle)
    sine = jnp.sin(angle)
    first = values[..., :half_width]
    second = values[..., half_width:]
    return jnp.concatenate(
        [first * cosine - second * sine, second * cosine + first * sine], axis=-1
    )


def head_norm(values, gain):
    scale = lax.rsqrt(jnp.mean(values * values, axis=-1, keepdims=True) + 1e-06)
    return values * scale * gain


TILE = 256


def contract_last(left, right):
    return lax.dot_general(
        left, right, (((1,), (1,)), ((), ())), preferred_element_type=jnp.float32
    )


def spread(block, axis, count, groups=None):
    copies = jnp.broadcast_to(block[None], (count,) + block.shape)
    return lax.all_to_all(copies, axis, 0, 0, tiled=True, axis_index_groups=groups)


def spread_mp(block):
    size = lax.axis_size("mp")
    groups = [list(range(core, size, 2)) for core in range(2)]
    own = spread(block, "mp", size // 2, groups)
    return own, lax.ppermute(own, "mp", [(i, i ^ 1) for i in range(size)])


def tiles(body, init=0):
    return lax.fori_loop(0, 1024 // TILE, body, init)


def place(core, own, other, target, start):
    for y in range(own.shape[0]):
        for part, at in ((own, core), (other, 1 - core)):
            first = pl.multiple_of((2 * y + at) * 128, 128)
            target[:, pl.ds(first, 128)] = part[y, :, start : start + 128]


def solve_kernel(
    core_ref, own, other, state, scale, gain, result,
    high, low, rho, rho_high, rho_low, image, way, way_image, total,
):
    core = core_ref[0]
    ridge = 0.125 * D
    place(core, own, other, high, 0)
    place(core, own, other, low, 128)

    def rows_of(i):
        return pl.ds(pl.multiple_of(i * TILE, TILE), TILE)

    def split(rows, value):
        rho[rows, :] = value
        top = value.astype(jnp.bfloat16)
        rho_high[rows, :] = top
        rho_low[rows, :] = (value - top.astype(jnp.float32)).astype(jnp.bfloat16)

    def start(i, carry):
        rows = rows_of(i)
        value = state[rows, :].astype(jnp.float32) * scale[rows, :] * gain[...]
        split(rows, value)
        way[rows, :] = value
        return carry

    tiles(start)

    def dot(left, right):
        return jnp.dot(left, right, preferred_element_type=jnp.float32)

    def product(i, square):
        rows = rows_of(i)
        value = dot(high[rows, :], rho_low[...]) + dot(low[rows, :], rho_high[...])
        value = value + dot(high[rows, :], rho_high[...])
        image[rows, :] = value
        return square + jnp.sum(rho[rows, :] * value, axis=0, keepdims=True)

    zero = jnp.zeros((1, state.shape[1]), jnp.float32)
    res_sq = tiles(product, zero)
    ratio = zero
    for sweep in range(ITERS):

        def turn(i, curvature):
            rows = rows_of(i)
            if sweep == 0:
                step, step_image = way[rows, :], image[rows, :]
            else:
                step = rho[rows, :] + ratio * way[rows, :]
                step_image = image[rows, :] + ratio * way_image[rows, :]
                way[rows, :] = step
            way_image[rows, :] = step_image
            return curvature + jnp.sum(
                step_image * (step_image + ridge * step), axis=0, keepdims=True
            )

        alpha = res_sq / tiles(turn, zero)

        def update(i, carry):
            rows = rows_of(i)
            step = way[rows, :]
            moved = alpha * step
            if sweep:
                moved = total[rows, :] + moved
            if sweep + 1 < ITERS:
                total[rows, :] = moved
                split(rows, rho[rows, :] - alpha * (way_image[rows, :] + ridge * step))
            else:
                result[rows, :] = moved.astype(jnp.bfloat16)
            return carry

        tiles(update)
        if sweep + 1 < ITERS:
            new_sq = tiles(product, zero)
            ratio = new_sq / res_sq
            res_sq = new_sq


def call(kernel, out_shape, scratch, operands, flops):
    vmem = pl.BlockSpec(memory_space=pltpu.VMEM)
    return pl.pallas_call(
        kernel,
        out_shape=out_shape,
        in_specs=[pl.BlockSpec(memory_space=pltpu.SMEM)] + [vmem] * (len(operands) - 1),
        out_specs=vmem,
        scratch_shapes=scratch,
        cost_estimate=pl.CostEstimate(flops=flops, bytes_accessed=1 << 23, transcendentals=0),
        compiler_params=pltpu.CompilerParams(vmem_limit_bytes=40 << 20),
    )(*operands)


def solve(*operands):
    anchors, cols = operands[3].shape
    wide = pltpu.VMEM((anchors, anchors), jnp.bfloat16)
    full = pltpu.VMEM((anchors, cols), jnp.float32)
    half = pltpu.VMEM((anchors, cols), jnp.bfloat16)
    return call(
        solve_kernel,
        jax.ShapeDtypeStruct((anchors, cols), jnp.bfloat16),
        [wide, wide, full, half, half, full, full, full, full],
        operands,
        18 * anchors * anchors * cols,
    )


def apply_kernel(core_ref, own, other, dual_map, result, routed):
    place(core_ref[0], own, other, routed, 0)

    def rows_of(i):
        return pl.ds(pl.multiple_of(i * TILE, TILE), TILE)

    def product(i, carry):
        rows = rows_of(i)
        value = jnp.dot(routed[rows, :], dual_map[...], preferred_element_type=jnp.float32)
        result[rows, :] = value.astype(jnp.bfloat16)
        return carry

    tiles(product)


def apply_map(*operands):
    anchors, cols = operands[3].shape
    slots = operands[1].shape[1]
    return call(
        apply_kernel,
        jax.ShapeDtypeStruct((slots, cols), jnp.bfloat16),
        [pltpu.VMEM((slots, anchors), jnp.bfloat16)],
        operands,
        2 * slots * anchors * cols,
    )


def local(
    hidden,
    attn_gain,
    w_query,
    w_key,
    w_value,
    w_output,
    query_gain,
    key_gain,
    key_cache,
    value_cache,
    lengths,
    final_gain,
    old_embed,
    slab,
    owners,
):
    docs = hidden.shape[0]
    width = hidden.shape[1]
    kv_local = w_key.shape[1] // HEAD
    group = HEADS // KV_HEADS
    rows_count = lax.axis_size("rows")
    mp_count = lax.axis_size("mp")
    cols = width // mp_count
    hidden32 = hidden.astype(jnp.float32)
    normed = (
        hidden32
        * lax.rsqrt(jnp.mean(hidden32 * hidden32, axis=-1, keepdims=True) + 1e-06)
        * attn_gain
    ).astype(jnp.bfloat16)
    position = lengths.astype(jnp.float32)
    query = jnp.dot(normed, w_query, preferred_element_type=jnp.float32).reshape(
        docs, kv_local * group, HEAD
    )
    query = rotate(head_norm(query, query_gain), position).astype(jnp.bfloat16)
    key_new = jnp.dot(normed, w_key, preferred_element_type=jnp.float32).reshape(
        docs, kv_local, HEAD
    )
    key_new = rotate(head_norm(key_new, key_gain), position).astype(jnp.bfloat16)
    value_new = (
        jnp.dot(normed, w_value, preferred_element_type=jnp.float32)
        .reshape(docs, kv_local, HEAD)
        .astype(jnp.bfloat16)
    )
    query_groups = query.reshape(docs, kv_local, group, HEAD)
    keys = key_cache.reshape(docs, key_cache.shape[1], kv_local, HEAD)
    values = value_cache.reshape(docs, value_cache.shape[1], kv_local, HEAD)
    scale = 1.0 / math.sqrt(HEAD)
    scores = (
        jnp.einsum("akgd,apkd->akgp", query_groups, keys, preferred_element_type=jnp.float32)
        * scale
    )
    own_score = (
        jnp.einsum("akgd,akd->akg", query_groups, key_new, preferred_element_type=jnp.float32)
        * scale
    )
    valid = jnp.arange(keys.shape[1], dtype=jnp.int32)[None, :] < lengths[:, None]
    scores = jnp.where(valid[:, None, None, :], scores, -jnp.inf)
    top = jnp.maximum(jnp.max(scores, axis=-1), own_score)
    expo = jnp.exp(scores - top[..., None])
    own_expo = jnp.exp(own_score - top)
    total = jnp.sum(expo, axis=-1) + own_expo
    weights = (expo / total[..., None]).astype(jnp.bfloat16)
    own_weight = (own_expo / total).astype(jnp.bfloat16)
    attended = jnp.einsum("akgp,apkd->akgd", weights, values, preferred_element_type=jnp.float32)
    attended = (
        attended
        + own_weight.astype(jnp.float32)[..., None] * value_new.astype(jnp.float32)[:, :, None, :]
    )
    attended = attended.reshape(docs, kv_local * group * HEAD).astype(jnp.bfloat16)
    partial_value = jnp.dot(attended, w_output, preferred_element_type=jnp.float32)
    mine = lax.axis_index("mp") * cols
    core = lax.axis_index("mp") % 2
    my_cols = lambda array, axis: lax.dynamic_slice_in_dim(array, mine, cols, axis)
    pieces = partial_value.astype(jnp.bfloat16).reshape(docs, mp_count, cols).transpose(1, 0, 2)
    pieces = lax.all_to_all(pieces, "mp", 0, 0, tiled=True)
    state = my_cols(hidden32, 1) + jnp.sum(pieces.astype(jnp.float32), axis=0)
    squares = jnp.sum(state * state, axis=-1)[None, :]
    squares = jnp.sum(spread(squares, "mp", mp_count), axis=0)
    scale_rows = lax.rsqrt(spread(squares, "rows", rows_count) / width + 1e-06)
    state_all = spread(state.astype(jnp.bfloat16), "rows", rows_count)

    old_mine = my_cols(old_embed, 1)
    old_all = spread(old_mine, "rows", rows_count).reshape(rows_count * docs, cols)
    anchors = rows_count * docs
    part = anchors // mp_count
    gram_part = contract_last(old_mine, old_all).reshape(docs, mp_count, part).transpose(1, 0, 2)
    gram_part = jnp.sum(lax.all_to_all(gram_part, "mp", 0, 0, tiled=True), axis=0)
    high = lax.reduce_precision(gram_part, 8, 7)
    gram_part = jnp.concatenate([high, gram_part - high], axis=1).astype(jnp.bfloat16)
    gram = spread(gram_part, "rows", rows_count).reshape(anchors, 2 * part)
    gram_own, gram_other = spread_mp(gram)

    slab_part = contract_last(slab, old_all).astype(jnp.bfloat16)
    slab_part = slab_part.reshape(-1, mp_count, part).transpose(1, 0, 2)
    slab_part = lax.all_to_all(slab_part, "mp", 0, 0, tiled=True)
    slab_dual = jnp.sum(slab_part.astype(jnp.float32), axis=0).astype(jnp.bfloat16)
    capacity = 2 * slab.shape[0] // rows_count
    owner_ids = owners[:, 0]
    onehot = (owner_ids[:, None] == jnp.arange(rows_count, dtype=jnp.int32)[None, :]).astype(
        jnp.int32
    )
    counted = jnp.cumsum(onehot, axis=0)
    slot = jnp.sum((counted - 1) * onehot, axis=-1)
    target = owner_ids * capacity + slot
    outgoing = jnp.zeros((rows_count * capacity, part), jnp.bfloat16).at[target].set(slab_dual)
    routed = lax.all_to_all(outgoing, "rows", split_axis=0, concat_axis=0, tiled=True)
    routed_own, routed_other = spread_mp(routed)

    core = core.astype(jnp.int32).reshape(1)
    dual_map = solve(
        core,
        gram_own,
        gram_other,
        state_all.reshape(anchors, cols),
        scale_rows.reshape(anchors, 1),
        my_cols(final_gain, 0).reshape(1, cols),
    )
    return apply_map(core, routed_own, routed_other, dual_map)


def solution(mesh):
    return jax.shard_map(
        local,
        mesh=mesh,
        in_specs=(
            P("rows", None),
            P(),
            P(None, "mp"),
            P(None, "mp"),
            P(None, "mp"),
            P("mp", None),
            P(),
            P(),
            P("rows", None, "mp"),
            P("rows", None, "mp"),
            P("rows"),
            P(),
            P("rows", None),
            P("rows", "mp"),
            P("rows", None),
        ),
        out_specs=P("rows", "mp"),
        check_vma=False,
    )
```

```python
import math

import jax
import jax.numpy as jnp
from jax import lax
from jax.experimental import pallas as pl
from jax.experimental.pallas import tpu as pltpu
from jax.sharding import PartitionSpec as P


D = 4096
HEADS = 32
KV_HEADS = 8
HEAD = 128
ITERS = 3


def rotate(values, position):
    half_width = values.shape[-1] // 2
    exponent = 2.0 * jnp.arange(half_width, dtype=jnp.float32) / values.shape[-1]
    frequency = jnp.exp(-exponent * math.log(1000000.0))
    angle = position[:, None, None] * frequency[None, None, :]
    cosine = jnp.cos(angle)
    sine = jnp.sin(angle)
    first = values[..., :half_width]
    second = values[..., half_width:]
    return jnp.concatenate(
        [first * cosine - second * sine, second * cosine + first * sine], axis=-1
    )


def head_norm(values, gain):
    scale = lax.rsqrt(jnp.mean(values * values, axis=-1, keepdims=True) + 1e-06)
    return values * scale * gain


TILE = 256


def contract_last(left, right):
    return lax.dot_general(
        left, right, (((1,), (1,)), ((), ())), preferred_element_type=jnp.float32
    )


def spread(block, axis, count, groups=None):
    copies = jnp.broadcast_to(block[None], (count,) + block.shape)
    return lax.all_to_all(copies, axis, 0, 0, tiled=True, axis_index_groups=groups)


def ring(block, axis, count, size, stride):
    def move(array, step):
        pairs = []
        for i in range(size):
            at = i // stride % count
            pairs.append((i, i + ((at + step) % count - at) * stride))
        return lax.ppermute(array, axis, pairs)

    below, above = [block], [block]
    for _ in range(count // 2 - 1):
        below.append(move(below[-1], 1))
        above.append(move(above[-1], -1))
    middle = block.shape[0] // 2
    far = [move(below[-1][:middle], 1), move(above[-1][middle:], -1)]
    far = jnp.concatenate(far, axis=0)
    return above + [far] + below[:0:-1]


def swap_cores(block, size):
    return lax.ppermute(block, "mp", [(i, i ^ 1) for i in range(size)])


def halves(array):
    high = lax.reduce_precision(array, 8, 7)
    return high.astype(jnp.bfloat16), (array - high).astype(jnp.bfloat16)


def norm_rows(squares, width):
    high, low = halves(squares)
    line = jnp.concatenate([high, low])
    return jnp.pad(line[None, :], ((0, 15), (0, width - line.shape[0])))


def tiles(body, init=0):
    return lax.fori_loop(0, 1024 // TILE, body, init)


def place(here, own, other, target, start, rows):
    core, chip = here[0], here[1]
    for step in range(own.shape[0]):
        at_chip = lax.rem(chip + step, own.shape[0])
        for part, at in ((own, core), (other, 1 - core)):
            first = pl.multiple_of((2 * at_chip + at) * 128, 128)
            value = part[step, :, start : start + rows, :]
            target[:, pl.ds(first, 128)] = value.reshape(target.shape[0], 128)


def solve_kernel(
    here, own, other, state, scale, gain, result,
    high, low, rho, rho_high, rho_low, image, way, way_image, total,
):
    ridge = 0.125 * D
    place(here, own, other, high, 0, own.shape[2] // 2)
    place(here, own, other, low, own.shape[2] // 2, own.shape[2] // 2)

    def rows_of(i):
        return pl.ds(pl.multiple_of(i * TILE, TILE), TILE)

    def split(rows, value):
        rho[rows, :] = value
        top = value.astype(jnp.bfloat16)
        rho_high[rows, :] = top
        rho_low[rows, :] = (value - top.astype(jnp.float32)).astype(jnp.bfloat16)

    def start(i, carry):
        rows = rows_of(i)
        value = state[rows, :].astype(jnp.float32) * scale[rows, :] * gain[...]
        split(rows, value)
        way[rows, :] = value
        return carry

    tiles(start)

    def dot(left, right):
        return jnp.dot(left, right, preferred_element_type=jnp.float32)

    def product(i, square):
        rows = rows_of(i)
        value = dot(high[rows, :], rho_low[...]) + dot(low[rows, :], rho_high[...])
        value = value + dot(high[rows, :], rho_high[...])
        image[rows, :] = value
        return square + jnp.sum(rho[rows, :] * value, axis=0, keepdims=True)

    zero = jnp.zeros((1, state.shape[1]), jnp.float32)
    res_sq = tiles(product, zero)
    ratio = zero
    for sweep in range(ITERS):

        def turn(i, curvature):
            rows = rows_of(i)
            if sweep == 0:
                step, step_image = way[rows, :], image[rows, :]
            else:
                step = rho[rows, :] + ratio * way[rows, :]
                step_image = image[rows, :] + ratio * way_image[rows, :]
                way[rows, :] = step
            way_image[rows, :] = step_image
            return curvature + jnp.sum(
                step_image * (step_image + ridge * step), axis=0, keepdims=True
            )

        alpha = res_sq / tiles(turn, zero)

        def update(i, carry):
            rows = rows_of(i)
            step = way[rows, :]
            moved = alpha * step
            if sweep:
                moved = total[rows, :] + moved
            if sweep + 1 < ITERS:
                total[rows, :] = moved
                split(rows, rho[rows, :] - alpha * (way_image[rows, :] + ridge * step))
            else:
                result[rows, :] = moved.astype(jnp.bfloat16)
            return carry

        tiles(update)
        if sweep + 1 < ITERS:
            new_sq = tiles(product, zero)
            ratio = new_sq / res_sq
            res_sq = new_sq


def call(kernel, out_shape, scratch, operands, flops):
    vmem = pl.BlockSpec(memory_space=pltpu.VMEM)
    return pl.pallas_call(
        kernel,
        out_shape=out_shape,
        in_specs=[pl.BlockSpec(memory_space=pltpu.SMEM)] + [vmem] * (len(operands) - 1),
        out_specs=vmem,
        scratch_shapes=scratch,
        cost_estimate=pl.CostEstimate(flops=flops, bytes_accessed=1 << 23, transcendentals=0),
        compiler_params=pltpu.CompilerParams(vmem_limit_bytes=40 << 20),
    )(*operands)


def solve(*operands):
    anchors, cols = operands[3].shape
    wide = pltpu.VMEM((anchors, anchors), jnp.bfloat16)
    full = pltpu.VMEM((anchors, cols), jnp.float32)
    half = pltpu.VMEM((anchors, cols), jnp.bfloat16)
    return call(
        solve_kernel,
        jax.ShapeDtypeStruct((anchors, cols), jnp.bfloat16),
        [wide, wide, full, half, half, full, full, full, full],
        operands,
        18 * anchors * anchors * cols,
    )


def apply_kernel(here, own, other, dual_map, result, routed):
    place(here, own, other, routed, 0, own.shape[2])

    def rows_of(i):
        return pl.ds(pl.multiple_of(i * TILE, TILE), TILE)

    def product(i, carry):
        rows = rows_of(i)
        value = jnp.dot(routed[rows, :], dual_map[...], preferred_element_type=jnp.float32)
        result[rows, :] = value.astype(jnp.bfloat16)
        return carry

    tiles(product)


def apply_map(*operands):
    anchors, cols = operands[3].shape
    slots = operands[1].shape[1] * operands[1].shape[2]
    return call(
        apply_kernel,
        jax.ShapeDtypeStruct((slots, cols), jnp.bfloat16),
        [pltpu.VMEM((slots, anchors), jnp.bfloat16)],
        operands,
        2 * slots * anchors * cols,
    )


def local(
    hidden,
    attn_gain,
    w_query,
    w_key,
    w_value,
    w_output,
    query_gain,
    key_gain,
    key_cache,
    value_cache,
    lengths,
    final_gain,
    old_embed,
    slab,
    owners,
):
    docs = hidden.shape[0]
    width = hidden.shape[1]
    kv_local = w_key.shape[1] // HEAD
    group = HEADS // KV_HEADS
    rows_count = lax.axis_size("rows")
    mp_count = lax.axis_size("mp")
    cols = width // mp_count
    hidden32 = hidden.astype(jnp.float32)
    normed = (
        hidden32
        * lax.rsqrt(jnp.mean(hidden32 * hidden32, axis=-1, keepdims=True) + 1e-06)
        * attn_gain
    ).astype(jnp.bfloat16)
    position = lengths.astype(jnp.float32)
    query = jnp.dot(normed, w_query, preferred_element_type=jnp.float32).reshape(
        docs, kv_local * group, HEAD
    )
    query = rotate(head_norm(query, query_gain), position).astype(jnp.bfloat16)
    key_new = jnp.dot(normed, w_key, preferred_element_type=jnp.float32).reshape(
        docs, kv_local, HEAD
    )
    key_new = rotate(head_norm(key_new, key_gain), position).astype(jnp.bfloat16)
    value_new = (
        jnp.dot(normed, w_value, preferred_element_type=jnp.float32)
        .reshape(docs, kv_local, HEAD)
        .astype(jnp.bfloat16)
    )
    query_groups = query.reshape(docs, kv_local, group, HEAD)
    keys = key_cache.reshape(docs, key_cache.shape[1], kv_local, HEAD)
    values = value_cache.reshape(docs, value_cache.shape[1], kv_local, HEAD)
    scale = 1.0 / math.sqrt(HEAD)
    scores = (
        jnp.einsum("akgd,apkd->akgp", query_groups, keys, preferred_element_type=jnp.float32)
        * scale
    )
    own_score = (
        jnp.einsum("akgd,akd->akg", query_groups, key_new, preferred_element_type=jnp.float32)
        * scale
    )
    valid = jnp.arange(keys.shape[1], dtype=jnp.int32)[None, :] < lengths[:, None]
    scores = jnp.where(valid[:, None, None, :], scores, -jnp.inf)
    top = jnp.maximum(jnp.max(scores, axis=-1), own_score)
    expo = jnp.exp(scores - top[..., None])
    own_expo = jnp.exp(own_score - top)
    total = jnp.sum(expo, axis=-1) + own_expo
    weights = (expo / total[..., None]).astype(jnp.bfloat16)
    own_weight = (own_expo / total).astype(jnp.bfloat16)
    attended = jnp.einsum("akgp,apkd->akgd", weights, values, preferred_element_type=jnp.float32)
    attended = (
        attended
        + own_weight.astype(jnp.float32)[..., None] * value_new.astype(jnp.float32)[:, :, None, :]
    )
    attended = attended.reshape(docs, kv_local * group * HEAD).astype(jnp.bfloat16)
    partial_value = lax.optimization_barrier(
        jnp.dot(attended, w_output, preferred_element_type=jnp.float32)
    )
    place_mp = lax.axis_index("mp")
    mine = place_mp * cols
    core, chip = place_mp % 2, place_mp // 2
    chips = mp_count // 2
    my_cols = lambda array, axis: lax.dynamic_slice_in_dim(array, mine, cols, axis)
    half = jnp.bfloat16

    def shift_chips(block, step):
        return lax.ppermute(
            block, "mp", [(i, (i + 2 * step) % mp_count) for i in range(mp_count)]
        )

    pieces = partial_value.reshape(docs, chips, 2, cols)
    theirs = lax.dynamic_index_in_dim(pieces, 1 - core, 2, False).astype(half)
    pieces = lax.dynamic_index_in_dim(pieces, core, 2, False)
    pieces = pieces + swap_cores(theirs, mp_count).astype(jnp.float32)
    state = my_cols(hidden32, 1) + lax.dynamic_index_in_dim(pieces, chip, 1, False)
    pieces = pieces.astype(half)
    for step in range(1, chips):
        piece = lax.dynamic_index_in_dim(pieces, (chip + step) % chips, 1, False)
        state = state + shift_chips(piece, step).astype(jnp.float32)
    squares = jnp.sum(state * state, axis=-1)

    old_mine = my_cols(old_embed, 1)
    old_all = spread(old_mine, "rows", rows_count).reshape(rows_count * docs, cols)
    anchors = rows_count * docs
    part = anchors // mp_count

    def by_part(array):
        return array.reshape(-1, mp_count, part).transpose(1, 0, 2)

    gram_part = by_part(contract_last(old_mine, old_all))
    slab_part = by_part(contract_last(slab, old_all).astype(half))
    count = slab.shape[0]
    head = count + 2 * docs
    outgoing = jnp.concatenate(
        [
            slab_part,
            *halves(gram_part),
            jnp.broadcast_to(norm_rows(squares, part)[None], (mp_count, 16, part)),
        ],
        axis=1,
    )
    summed = jnp.sum(lax.all_to_all(outgoing, "mp", 0, 0, tiled=True).astype(jnp.float32), axis=0)
    slab_dual = summed[:count].astype(half)
    gram_part = summed[count : count + docs] + summed[count + docs : head]
    squares = summed[head, :docs] + summed[head, docs : 2 * docs]

    capacity = 2 * count // rows_count
    owner_ids = owners[:, 0]
    onehot = (owner_ids[:, None] == jnp.arange(rows_count, dtype=jnp.int32)[None, :]).astype(
        jnp.int32
    )
    counted = jnp.cumsum(onehot, axis=0)
    slot = jnp.sum((counted - 1) * onehot, axis=-1)
    target = owner_ids * capacity + slot
    routed = jnp.zeros((rows_count * capacity, part), half).at[target].set(slab_dual)
    shared = jnp.concatenate([*halves(gram_part), norm_rows(squares, part)], axis=0)
    outgoing = jnp.concatenate(
        [
            routed.reshape(rows_count, capacity, part),
            jnp.broadcast_to(shared[None], (rows_count,) + shared.shape),
        ],
        axis=1,
    )
    arrived = lax.all_to_all(outgoing, "rows", split_axis=0, concat_axis=0, tiled=True)
    routed = arrived[:, :capacity]
    gram = arrived[:, capacity : capacity + 2 * docs]
    squares = arrived[:, capacity + 2 * docs].astype(jnp.float32)
    squares = squares[:, :docs] + squares[:, docs : 2 * docs]
    scale_rows = lax.rsqrt(squares / width + 1e-06).reshape(anchors, 1)

    state, _ = lax.optimization_barrier((state.astype(half), arrived))
    state_all = spread(state, "rows", rows_count)
    gram_own = jnp.stack(ring(gram, "mp", chips, mp_count, 2))
    gram_other = swap_cores(gram_own, mp_count)
    routed, _ = lax.optimization_barrier((routed, state_all))
    routed_own = spread(
        routed, "mp", chips, [list(range(at, mp_count, 2)) for at in range(2)]
    )
    routed_other = swap_cores(routed_own, mp_count)

    here = jnp.stack([core, chip]).astype(jnp.int32)
    dual_map = solve(
        here,
        gram_own,
        gram_other,
        state_all.reshape(anchors, cols),
        scale_rows,
        my_cols(final_gain, 0).reshape(1, cols),
    )
    return apply_map(here * jnp.array([1, 0], jnp.int32), routed_own, routed_other, dual_map)


def solution(mesh):
    return jax.shard_map(
        local,
        mesh=mesh,
        in_specs=(
            P("rows", None),
            P(),
            P(None, "mp"),
            P(None, "mp"),
            P(None, "mp"),
            P("mp", None),
            P(),
            P(),
            P("rows", None, "mp"),
            P("rows", None, "mp"),
            P("rows"),
            P(),
            P("rows", None),
            P("rows", "mp"),
            P("rows", None),
        ),
        out_specs=P("rows", "mp"),
        check_vma=False,
    )
```

```python
import math

import jax
import jax.numpy as jnp
from jax import lax
from jax.experimental import pallas as pl
from jax.experimental.pallas import tpu as pltpu
from jax.sharding import PartitionSpec as P


D = 4096
HEADS = 32
KV_HEADS = 8
HEAD = 128
ITERS = 3


def rotate(values, position):
    half_width = values.shape[-1] // 2
    exponent = 2.0 * jnp.arange(half_width, dtype=jnp.float32) / values.shape[-1]
    frequency = jnp.exp(-exponent * math.log(1000000.0))
    angle = position[:, None, None] * frequency[None, None, :]
    cosine = jnp.cos(angle)
    sine = jnp.sin(angle)
    first = values[..., :half_width]
    second = values[..., half_width:]
    return jnp.concatenate(
        [first * cosine - second * sine, second * cosine + first * sine], axis=-1
    )


def head_norm(values, gain):
    scale = lax.rsqrt(jnp.mean(values * values, axis=-1, keepdims=True) + 1e-06)
    return values * scale * gain


TILE = 256


def contract_last(left, right):
    return lax.dot_general(
        left, right, (((1,), (1,)), ((), ())), preferred_element_type=jnp.float32
    )


def spread(block, axis, count, groups=None):
    copies = jnp.broadcast_to(block[None], (count,) + block.shape)
    return lax.all_to_all(copies, axis, 0, 0, tiled=True, axis_index_groups=groups)


def ring(block, axis, count, size, stride):
    def move(array, step):
        pairs = []
        for i in range(size):
            at = i // stride % count
            pairs.append((i, i + ((at + step) % count - at) * stride))
        return lax.ppermute(array, axis, pairs)

    below, above = [block], [block]
    for _ in range(count // 2 - 1):
        below.append(move(below[-1], 1))
        above.append(move(above[-1], -1))
    middle = block.shape[0] // 2
    far = [move(below[-1][:middle], 1), move(above[-1][middle:], -1)]
    return above + below[:0:-1] + far


def swap_cores(block, size):
    return lax.ppermute(block, "mp", [(i, i ^ 1) for i in range(size)])


def halves(array):
    high = lax.reduce_precision(array, 8, 7)
    return high.astype(jnp.bfloat16), (array - high).astype(jnp.bfloat16)


def norm_rows(squares, width):
    high, low = halves(squares)
    line = jnp.concatenate([high, low])
    return jnp.pad(line[None, :], ((0, 15), (0, width - line.shape[0])))


def tiles(body, init=0):
    return lax.fori_loop(0, 1024 // TILE, body, init)


def put(block, target, place, row=0):
    first = pl.multiple_of(place * 128, 128)
    value = block.reshape(block.shape[0] * block.shape[1], 128)
    target[row : row + value.shape[0], pl.ds(first, 128)] = value


def solve_kernel(here, scale, gain, *refs):
    states, grams, result = refs[:4], refs[4:14], refs[14]
    high, low, rho, rho_high, rho_low, image, way, way_image, total = refs[15:]
    ridge = 0.125 * D
    for index, piece in enumerate(grams):
        step, row = ((0, 0), (1, 0), (3, 0), (2, 0), (2, 512))[index % 5]
        side = here[0] if index < 5 else 1 - here[0]
        at = 2 * lax.rem(here[1] + step, 4) + side
        docs = piece.shape[1] // 2
        put(piece[:, :docs, :], high, at, row)
        put(piece[:, docs:, :], low, at, row)

    def rows_of(i):
        return pl.ds(pl.multiple_of(i * TILE, TILE), TILE)

    def split(rows, value):
        rho[rows, :] = value
        top = value.astype(jnp.bfloat16)
        rho_high[rows, :] = top
        rho_low[rows, :] = (value - top.astype(jnp.float32)).astype(jnp.bfloat16)

    for step, state in enumerate(states):
        rows = rows_of(lax.rem(here[2] + step, 4))
        value = state[...].astype(jnp.float32) * scale[rows, :] * gain[...]
        split(rows, value)
        way[rows, :] = value

    def dot(left, right):
        return jnp.dot(left, right, preferred_element_type=jnp.float32)

    def product(i, square):
        rows = rows_of(i)
        value = dot(high[rows, :], rho_low[...]) + dot(low[rows, :], rho_high[...])
        value = value + dot(high[rows, :], rho_high[...])
        image[rows, :] = value
        return square + jnp.sum(rho[rows, :] * value, axis=0, keepdims=True)

    zero = jnp.zeros((1, rho.shape[1]), jnp.float32)
    res_sq = tiles(product, zero)
    ratio = zero
    for sweep in range(ITERS):

        def turn(i, curvature):
            rows = rows_of(i)
            if sweep == 0:
                step, step_image = way[rows, :], image[rows, :]
            else:
                step = rho[rows, :] + ratio * way[rows, :]
                step_image = image[rows, :] + ratio * way_image[rows, :]
                way[rows, :] = step
            way_image[rows, :] = step_image
            return curvature + jnp.sum(
                step_image * (step_image + ridge * step), axis=0, keepdims=True
            )

        alpha = res_sq / tiles(turn, zero)

        def update(i, carry):
            rows = rows_of(i)
            step = way[rows, :]
            moved = alpha * step
            if sweep:
                moved = total[rows, :] + moved
            if sweep + 1 < ITERS:
                total[rows, :] = moved
                split(rows, rho[rows, :] - alpha * (way_image[rows, :] + ridge * step))
            else:
                result[rows, :] = moved.astype(jnp.bfloat16)
            return carry

        tiles(update)
        if sweep + 1 < ITERS:
            new_sq = tiles(product, zero)
            ratio = new_sq / res_sq
            res_sq = new_sq


def call(kernel, out_shape, scratch, operands, flops):
    vmem = pl.BlockSpec(memory_space=pltpu.VMEM)
    return pl.pallas_call(
        kernel,
        out_shape=out_shape,
        in_specs=[pl.BlockSpec(memory_space=pltpu.SMEM)] + [vmem] * (len(operands) - 1),
        out_specs=vmem,
        scratch_shapes=scratch,
        cost_estimate=pl.CostEstimate(flops=flops, bytes_accessed=1 << 23, transcendentals=0),
        compiler_params=pltpu.CompilerParams(vmem_limit_bytes=32 << 20),
    )(*operands)


def solve(*operands):
    anchors, cols = operands[1].shape[0], operands[2].shape[1]
    wide = pltpu.VMEM((anchors, anchors), jnp.bfloat16)
    full = pltpu.VMEM((anchors, cols), jnp.float32)
    half = pltpu.VMEM((anchors, cols), jnp.bfloat16)
    return call(
        solve_kernel,
        jax.ShapeDtypeStruct((anchors, cols), jnp.bfloat16),
        [wide, wide, full, half, half, full, full, full, full],
        operands,
        18 * anchors * anchors * cols,
    )


def apply_kernel(here, own, other, dual_map, result, routed):
    for y in range(own.shape[0]):
        put(own[y], routed, 2 * y + here[0])
        put(other[y], routed, 2 * y + 1 - here[0])

    def rows_of(i):
        return pl.ds(pl.multiple_of(i * TILE, TILE), TILE)

    def product(i, carry):
        rows = rows_of(i)
        value = jnp.dot(routed[rows, :], dual_map[...], preferred_element_type=jnp.float32)
        result[rows, :] = value.astype(jnp.bfloat16)
        return carry

    tiles(product)


def apply_map(*operands):
    anchors, cols = operands[3].shape
    slots = operands[1].shape[1] * operands[1].shape[2]
    return call(
        apply_kernel,
        jax.ShapeDtypeStruct((slots, cols), jnp.bfloat16),
        [pltpu.VMEM((slots, anchors), jnp.bfloat16)],
        operands,
        2 * slots * anchors * cols,
    )


def local(
    hidden,
    attn_gain,
    w_query,
    w_key,
    w_value,
    w_output,
    query_gain,
    key_gain,
    key_cache,
    value_cache,
    lengths,
    final_gain,
    old_embed,
    slab,
    owners,
):
    docs = hidden.shape[0]
    width = hidden.shape[1]
    kv_local = w_key.shape[1] // HEAD
    group = HEADS // KV_HEADS
    rows_count = lax.axis_size("rows")
    mp_count = lax.axis_size("mp")
    cols = width // mp_count
    hidden32 = hidden.astype(jnp.float32)
    normed = (
        hidden32
        * lax.rsqrt(jnp.mean(hidden32 * hidden32, axis=-1, keepdims=True) + 1e-06)
        * attn_gain
    ).astype(jnp.bfloat16)
    position = lengths.astype(jnp.float32)
    query = jnp.dot(normed, w_query, preferred_element_type=jnp.float32).reshape(
        docs, kv_local * group, HEAD
    )
    key_new = jnp.dot(normed, w_key, preferred_element_type=jnp.float32).reshape(
        docs, kv_local, HEAD
    )
    value_new = (
        jnp.dot(normed, w_value, preferred_element_type=jnp.float32)
        .reshape(docs, kv_local, HEAD)
        .astype(jnp.bfloat16)
    )
    query = rotate(head_norm(query, query_gain), position).astype(jnp.bfloat16)
    key_new = rotate(head_norm(key_new, key_gain), position).astype(jnp.bfloat16)
    query_groups = query.reshape(docs, kv_local, group, HEAD)
    keys = key_cache.reshape(docs, key_cache.shape[1], kv_local, HEAD)
    values = value_cache.reshape(docs, value_cache.shape[1], kv_local, HEAD)
    scale = 1.0 / math.sqrt(HEAD)
    scores = (
        jnp.einsum("akgd,apkd->akgp", query_groups, keys, preferred_element_type=jnp.float32)
        * scale
    )
    own_score = (
        jnp.einsum("akgd,akd->akg", query_groups, key_new, preferred_element_type=jnp.float32)
        * scale
    )
    valid = jnp.arange(keys.shape[1], dtype=jnp.int32)[None, :] < lengths[:, None]
    scores = jnp.where(valid[:, None, None, :], scores, -jnp.inf)
    top = jnp.maximum(jnp.max(scores, axis=-1), own_score)
    expo = jnp.exp(scores - top[..., None])
    own_expo = jnp.exp(own_score - top)
    total = jnp.sum(expo, axis=-1) + own_expo
    weights = (expo / total[..., None]).astype(jnp.bfloat16)
    own_weight = (own_expo / total).astype(jnp.bfloat16)
    attended = jnp.einsum("akgp,apkd->akgd", weights, values, preferred_element_type=jnp.float32)
    attended = (
        attended
        + own_weight.astype(jnp.float32)[..., None] * value_new.astype(jnp.float32)[:, :, None, :]
    )
    attended = attended.reshape(docs, kv_local * group * HEAD).astype(jnp.bfloat16)
    partial_value = lax.optimization_barrier(
        jnp.dot(attended, w_output, preferred_element_type=jnp.float32)
    )
    place_mp = lax.axis_index("mp")
    mine = place_mp * cols
    core, chip = place_mp % 2, place_mp // 2
    chips = mp_count // 2
    my_cols = lambda array, axis: lax.dynamic_slice_in_dim(array, mine, cols, axis)
    half = jnp.bfloat16

    def shift_chips(block, step):
        return lax.ppermute(
            block, "mp", [(i, (i + 2 * step) % mp_count) for i in range(mp_count)]
        )

    pieces = partial_value.reshape(docs, chips, 2, cols)
    theirs = lax.dynamic_index_in_dim(pieces, 1 - core, 2, False).astype(half)
    pieces = lax.dynamic_index_in_dim(pieces, core, 2, False)
    pieces = pieces + swap_cores(theirs, mp_count).astype(jnp.float32)
    state = my_cols(hidden32, 1) + lax.dynamic_index_in_dim(pieces, chip, 1, False)
    pieces = pieces.astype(half)
    for step in range(1, chips):
        piece = lax.dynamic_index_in_dim(pieces, (chip + step) % chips, 1, False)
        state = state + shift_chips(piece, step).astype(jnp.float32)
    squares = jnp.sum(state * state, axis=-1)

    line = 4
    column = rows_count // line
    by_z = [[x + line * z for z in range(column)] for x in range(line)]
    by_x = [[x + line * z for x in range(line)] for z in range(column)]
    by_y = [list(range(at, mp_count, 2)) for at in range(2)]
    old_mine = my_cols(old_embed, 1)
    old_all = spread(old_mine, "rows", column, by_z)
    old_all = spread(old_all, "rows", line, by_x)
    anchors = rows_count * docs
    part = anchors // mp_count
    old_all = old_all.reshape(anchors, cols)

    def by_part(array):
        return array.reshape(-1, mp_count, part).transpose(1, 0, 2)

    gram_part = by_part(contract_last(old_mine, old_all))
    gram_part = lax.all_to_all(gram_part, "mp", 0, 0, tiled=True)
    gram = jnp.concatenate(halves(jnp.sum(gram_part, axis=0)), axis=0)
    gram = spread(gram, "rows", column, by_z)
    gram = spread(gram, "rows", line, by_x)
    gram = gram.reshape(rows_count, 2 * docs, part)

    count = slab.shape[0]
    slab_part = by_part(contract_last(slab, old_all).astype(half))
    slab_part = slab_part.reshape(chips, 2, count, part)
    theirs = lax.dynamic_index_in_dim(slab_part, 1 - core, 1, False)
    slab_part = lax.dynamic_index_in_dim(slab_part, core, 1, False).astype(jnp.float32)
    theirs, others = jnp.split(
        swap_cores(
            jnp.concatenate(
                [theirs.reshape(chips * count, part), norm_rows(squares, part)], axis=0
            ),
            mp_count,
        ).astype(jnp.float32),
        [chips * count],
    )
    slab_part = slab_part + theirs.reshape(chips, count, part)
    squares = squares + others[0, :docs] + others[0, docs : 2 * docs]
    slab_dual = lax.dynamic_index_in_dim(slab_part, chip, 0, False)
    slab_part = slab_part.astype(half)
    pair_rows = norm_rows(squares, part)
    for step in range(1, chips):
        piece = lax.dynamic_index_in_dim(slab_part, (chip + step) % chips, 0, False)
        piece = shift_chips(jnp.concatenate([piece, pair_rows], axis=0), step)
        piece = piece.astype(jnp.float32)
        slab_dual = slab_dual + piece[:count]
        squares = squares + piece[count, :docs] + piece[count, docs : 2 * docs]

    capacity = 2 * count // rows_count
    owner_ids = owners[:, 0]
    onehot = (owner_ids[:, None] == jnp.arange(rows_count, dtype=jnp.int32)[None, :]).astype(
        jnp.int32
    )
    counted = jnp.cumsum(onehot, axis=0)
    slot = jnp.sum((counted - 1) * onehot, axis=-1)
    target = owner_ids * capacity + slot
    routed = jnp.zeros((rows_count * capacity, part), half).at[target].set(slab_dual.astype(half))
    outgoing = jnp.concatenate(
        [
            routed.reshape(rows_count, capacity, part),
            jnp.broadcast_to(norm_rows(squares, part)[None], (rows_count, 16, part)),
        ],
        axis=1,
    )

    state, gram = lax.optimization_barrier((state.astype(half), gram))
    state_column = spread(state, "rows", column, by_z)
    outgoing, state_column = lax.optimization_barrier((outgoing, state_column))
    arrived = lax.all_to_all(outgoing, "rows", split_axis=0, concat_axis=0, tiled=True)
    states = [state_column.reshape(anchors // line, cols)]
    for step in range(1, line):
        pairs = [(i, i // line * line + (i - step) % line) for i in range(rows_count)]
        states.append(lax.ppermute(states[0], "rows", pairs))
    routed = arrived[:, :capacity]
    squares = arrived[:, capacity].astype(jnp.float32)
    squares = squares[:, :docs] + squares[:, docs : 2 * docs]
    squares = squares.reshape(column, line, docs).transpose(1, 0, 2)
    scale_rows = lax.rsqrt(squares / width + 1e-06).reshape(anchors, 1)

    grams = ring(gram, "mp", chips, mp_count, 2)
    grams = grams + [swap_cores(piece, mp_count) for piece in grams]
    routed_own = spread(routed, "mp", chips, by_y)
    routed_other = swap_cores(routed_own, mp_count)

    zero = jnp.zeros_like(core)
    here = jnp.stack([core, chip, lax.axis_index("rows") % line, zero]).astype(jnp.int32)
    dual_map = solve(
        here, scale_rows, my_cols(final_gain, 0).reshape(1, cols), *states, *grams
    )
    return apply_map(here, routed_own, routed_other, dual_map)


def solution(mesh):
    return jax.shard_map(
        local,
        mesh=mesh,
        in_specs=(
            P("rows", None),
            P(),
            P(None, "mp"),
            P(None, "mp"),
            P(None, "mp"),
            P("mp", None),
            P(),
            P(),
            P("rows", None, "mp"),
            P("rows", None, "mp"),
            P("rows"),
            P(),
            P("rows", None),
            P("rows", "mp"),
            P("rows", None),
        ),
        out_specs=P("rows", "mp"),
        check_vma=False,
    )
```

```python
import math

import jax
import jax.numpy as jnp
from jax import lax
from jax.experimental import pallas as pl
from jax.experimental.pallas import tpu as pltpu
from jax.sharding import PartitionSpec as P


D = 4096
HEADS = 32
KV_HEADS = 8
HEAD = 128
ITERS = 3


def rotate(values, position):
    half_width = values.shape[-1] // 2
    exponent = 2.0 * jnp.arange(half_width, dtype=jnp.float32) / values.shape[-1]
    frequency = jnp.exp(-exponent * math.log(1000000.0))
    angle = position[:, None, None] * frequency[None, None, :]
    cosine = jnp.cos(angle)
    sine = jnp.sin(angle)
    first = values[..., :half_width]
    second = values[..., half_width:]
    return jnp.concatenate(
        [first * cosine - second * sine, second * cosine + first * sine], axis=-1
    )


def head_norm(values, gain):
    scale = lax.rsqrt(jnp.mean(values * values, axis=-1, keepdims=True) + 1e-06)
    return values * scale * gain


TILE = 256
SMEM = pl.BlockSpec(memory_space=pltpu.SMEM)
VMEM = pl.BlockSpec(memory_space=pltpu.VMEM)
ANY = pl.BlockSpec(memory_space=pl.ANY)


def contract_last(left, right):
    return lax.dot_general(
        left, right, (((1,), (1,)), ((), ())), preferred_element_type=jnp.float32
    )


def spread(block, axis, count, groups=None):
    copies = jnp.broadcast_to(block[None], (count,) + block.shape)
    return lax.all_to_all(copies, axis, 0, 0, tiled=True, axis_index_groups=groups)


def ring(block, axis, count, size, stride):
    def move(array, step):
        pairs = []
        for i in range(size):
            at = i // stride % count
            pairs.append((i, i + ((at + step) % count - at) * stride))
        return lax.ppermute(array, axis, pairs)

    below, above = [block], [block]
    for _ in range(count // 2 - 1):
        below.append(move(below[-1], 1))
        above.append(move(above[-1], -1))
    middle = block.shape[0] // 2
    far = [move(below[-1][:middle], 1), move(above[-1][middle:], -1)]
    return above + below[:0:-1] + far


def swap_cores(block, size):
    return lax.ppermute(block, "mp", [(i, i ^ 1) for i in range(size)])


def halves(array):
    high = lax.reduce_precision(array, 8, 7)
    return high.astype(jnp.bfloat16), (array - high).astype(jnp.bfloat16)


def norm_rows(squares, width):
    high, low = halves(squares)
    line = jnp.concatenate([high, low])
    return jnp.pad(line[None, :], ((0, 15), (0, width - line.shape[0])))


def tiles(body, init=0):
    return lax.fori_loop(0, 1024 // TILE, body, init)


def columns(place):
    return pl.ds(pl.multiple_of(place * 128, 128), 128)


def copy_all(pairs, sems):
    copies = [pltpu.make_async_copy(a, b, sems.at[i]) for i, (a, b) in enumerate(pairs)]
    for copy in copies:
        copy.start()
    return copies


def solve_kernel(here, scale, gain, *refs):
    states, grams, result = refs[:4], refs[4:14], refs[14]
    state, high, low, rho, rho_high, rho_low, image, way, way_image, total = refs[15:25]
    state_sems, gram_sems = refs[25:]
    ridge = 0.125 * D
    placed = [
        (piece, state.at[:, lax.rem(here[2] + step, 4)]) for step, piece in enumerate(states)
    ]
    state_copies = copy_all(placed, state_sems)
    placed = []
    for index, piece in enumerate(grams):
        step, row = ((0, 0), (1, 0), (3, 0), (2, 0), (2, 16))[index % 5]
        side = here[0] if index < 5 else 1 - here[0]
        at = columns(2 * lax.rem(here[1] + step, 4) + side)
        docs = piece.shape[1] // 2
        rows = slice(row, row + piece.shape[0])
        placed.append((piece.at[:, :docs], high.at[rows, :, at]))
        placed.append((piece.at[:, docs:], low.at[rows, :, at]))
    gram_copies = copy_all(placed, gram_sems)
    for copy in state_copies:
        copy.wait()

    def rows_of(i):
        return pl.ds(pl.multiple_of(i * TILE, TILE), TILE)

    def split(rows, value):
        rho[rows, :] = value
        top = value.astype(jnp.bfloat16)
        rho_high[rows, :] = top
        rho_low[rows, :] = (value - top.astype(jnp.float32)).astype(jnp.bfloat16)

    def start(i, carry):
        rows = rows_of(i)
        value = state[pl.ds(2 * i, 2)].reshape(TILE, -1).astype(jnp.float32)
        value = value * scale[rows, :] * gain[...]
        split(rows, value)
        way[rows, :] = value
        return carry

    tiles(start)
    for copy in gram_copies:
        copy.wait()

    def gram_rows(block, i):
        return block[pl.ds(8 * i, 8)].reshape(TILE, -1)

    def dot(left, right):
        return jnp.dot(left, right, preferred_element_type=jnp.float32)

    def product(i, square):
        rows = rows_of(i)
        top = gram_rows(high, i)
        value = dot(top, rho_low[...]) + dot(gram_rows(low, i), rho_high[...])
        value = value + dot(top, rho_high[...])
        image[rows, :] = value
        return square + jnp.sum(rho[rows, :] * value, axis=0, keepdims=True)

    zero = jnp.zeros((1, rho.shape[1]), jnp.float32)
    res_sq = tiles(product, zero)
    ratio = zero
    for sweep in range(ITERS):

        def turn(i, curvature):
            rows = rows_of(i)
            if sweep == 0:
                step, step_image = way[rows, :], image[rows, :]
            else:
                step = rho[rows, :] + ratio * way[rows, :]
                step_image = image[rows, :] + ratio * way_image[rows, :]
                way[rows, :] = step
            way_image[rows, :] = step_image
            return curvature + jnp.sum(
                step_image * (step_image + ridge * step), axis=0, keepdims=True
            )

        alpha = res_sq / tiles(turn, zero)

        def update(i, carry):
            rows = rows_of(i)
            step = way[rows, :]
            moved = alpha * step
            if sweep:
                moved = total[rows, :] + moved
            if sweep + 1 < ITERS:
                total[rows, :] = moved
                split(rows, rho[rows, :] - alpha * (way_image[rows, :] + ridge * step))
            else:
                result[rows, :] = moved.astype(jnp.bfloat16)
            return carry

        tiles(update)
        if sweep + 1 < ITERS:
            new_sq = tiles(product, zero)
            ratio = new_sq / res_sq
            res_sq = new_sq


def call(kernel, out_shape, in_specs, scratch, operands, flops):
    return pl.pallas_call(
        kernel,
        out_shape=out_shape,
        in_specs=in_specs,
        out_specs=VMEM,
        scratch_shapes=scratch,
        cost_estimate=pl.CostEstimate(flops=flops, bytes_accessed=1 << 23, transcendentals=0),
        compiler_params=pltpu.CompilerParams(vmem_limit_bytes=62 << 20),
    )(*operands)


def solve(*operands):
    anchors, cols = operands[1].shape[0], operands[2].shape[1]
    wide = pltpu.VMEM((32, anchors // 32, anchors), jnp.bfloat16)
    full = pltpu.VMEM((anchors, cols), jnp.float32)
    half = pltpu.VMEM((anchors, cols), jnp.bfloat16)
    return call(
        solve_kernel,
        jax.ShapeDtypeStruct((anchors, cols), jnp.bfloat16),
        [SMEM, VMEM, VMEM] + [ANY] * 14,
        [pltpu.VMEM((8, 4, anchors // 32, cols), jnp.bfloat16), wide, wide, full, half, half]
        + [full] * 4
        + [pltpu.SemaphoreType.DMA((4,)), pltpu.SemaphoreType.DMA((20,))],
        operands,
        18 * anchors * anchors * cols,
    )


def apply_kernel(here, own, other, dual_map, result, routed, sems):
    placed = []
    for y in range(4):
        placed.append((own.at[y], routed.at[:, :, columns(2 * y + here[0])]))
        placed.append((other.at[y], routed.at[:, :, columns(2 * y + 1 - here[0])]))
    for copy in copy_all(placed, sems):
        copy.wait()

    def product(i, carry):
        rows = routed[pl.ds(8 * i, 8)].reshape(TILE, -1)
        value = jnp.dot(rows, dual_map[...], preferred_element_type=jnp.float32)
        result[pl.ds(pl.multiple_of(i * TILE, TILE), TILE), :] = value.astype(jnp.bfloat16)
        return carry

    tiles(product)


def apply_map(*operands):
    anchors, cols = operands[3].shape
    blocks, slots = operands[1].shape[1:3]
    return call(
        apply_kernel,
        jax.ShapeDtypeStruct((blocks * slots, cols), jnp.bfloat16),
        [SMEM, ANY, ANY, VMEM],
        [
            pltpu.VMEM((blocks, slots, anchors), jnp.bfloat16),
            pltpu.SemaphoreType.DMA((8,)),
        ],
        operands,
        2 * anchors * anchors * cols,
    )


def local(
    hidden,
    attn_gain,
    w_query,
    w_key,
    w_value,
    w_output,
    query_gain,
    key_gain,
    key_cache,
    value_cache,
    lengths,
    final_gain,
    old_embed,
    slab,
    owners,
):
    docs = hidden.shape[0]
    width = hidden.shape[1]
    kv_local = w_key.shape[1] // HEAD
    group = HEADS // KV_HEADS
    rows_count = lax.axis_size("rows")
    mp_count = lax.axis_size("mp")
    cols = width // mp_count
    hidden32 = hidden.astype(jnp.float32)
    normed = (
        hidden32
        * lax.rsqrt(jnp.mean(hidden32 * hidden32, axis=-1, keepdims=True) + 1e-06)
        * attn_gain
    ).astype(jnp.bfloat16)
    position = lengths.astype(jnp.float32)
    query = jnp.dot(normed, w_query, preferred_element_type=jnp.float32).reshape(
        docs, kv_local * group, HEAD
    )
    key_new = jnp.dot(normed, w_key, preferred_element_type=jnp.float32).reshape(
        docs, kv_local, HEAD
    )
    value_new = (
        jnp.dot(normed, w_value, preferred_element_type=jnp.float32)
        .reshape(docs, kv_local, HEAD)
        .astype(jnp.bfloat16)
    )
    query = rotate(head_norm(query, query_gain), position).astype(jnp.bfloat16)
    key_new = rotate(head_norm(key_new, key_gain), position).astype(jnp.bfloat16)
    query_groups = query.reshape(docs, kv_local, group, HEAD)
    keys = key_cache.reshape(docs, key_cache.shape[1], kv_local, HEAD)
    values = value_cache.reshape(docs, value_cache.shape[1], kv_local, HEAD)
    scale = 1.0 / math.sqrt(HEAD)
    scores = (
        jnp.einsum("akgd,apkd->akgp", query_groups, keys, preferred_element_type=jnp.float32)
        * scale
    )
    own_score = (
        jnp.einsum("akgd,akd->akg", query_groups, key_new, preferred_element_type=jnp.float32)
        * scale
    )
    valid = jnp.arange(keys.shape[1], dtype=jnp.int32)[None, :] < lengths[:, None]
    scores = jnp.where(valid[:, None, None, :], scores, -jnp.inf)
    top = jnp.maximum(jnp.max(scores, axis=-1), own_score)
    expo = jnp.exp(scores - top[..., None])
    own_expo = jnp.exp(own_score - top)
    total = jnp.sum(expo, axis=-1) + own_expo
    weights = (expo / total[..., None]).astype(jnp.bfloat16)
    own_weight = (own_expo / total).astype(jnp.bfloat16)
    attended = jnp.einsum("akgp,apkd->akgd", weights, values, preferred_element_type=jnp.float32)
    attended = (
        attended
        + own_weight.astype(jnp.float32)[..., None] * value_new.astype(jnp.float32)[:, :, None, :]
    )
    attended = attended.reshape(docs, kv_local * group * HEAD).astype(jnp.bfloat16)
    partial_value = lax.optimization_barrier(
        jnp.dot(attended, w_output, preferred_element_type=jnp.float32)
    )
    place_mp = lax.axis_index("mp")
    mine = place_mp * cols
    core, chip = place_mp % 2, place_mp // 2
    chips = mp_count // 2
    my_cols = lambda array, axis: lax.dynamic_slice_in_dim(array, mine, cols, axis)
    half = jnp.bfloat16

    def shift_chips(block, step):
        return lax.ppermute(
            block, "mp", [(i, (i + 2 * step) % mp_count) for i in range(mp_count)]
        )

    pieces = partial_value.reshape(docs, chips, 2, cols)
    theirs = lax.dynamic_index_in_dim(pieces, 1 - core, 2, False).astype(half)
    pieces = lax.dynamic_index_in_dim(pieces, core, 2, False)
    pieces = pieces + swap_cores(theirs, mp_count).astype(jnp.float32)
    state = my_cols(hidden32, 1) + lax.dynamic_index_in_dim(pieces, chip, 1, False)
    pieces = pieces.astype(half)
    for step in range(1, chips):
        piece = lax.dynamic_index_in_dim(pieces, (chip + step) % chips, 1, False)
        state = state + shift_chips(piece, step).astype(jnp.float32)
    squares = jnp.sum(state * state, axis=-1)

    line = 4
    column = rows_count // line
    by_z = [[x + line * z for z in range(column)] for x in range(line)]
    by_y = [list(range(at, mp_count, 2)) for at in range(2)]
    old_mine = my_cols(old_embed, 1)
    old_all = spread(old_mine, "rows", rows_count)
    anchors = rows_count * docs
    part = anchors // mp_count
    old_all = old_all.reshape(anchors, cols)

    def by_part(array):
        return array.reshape(-1, mp_count, part).transpose(1, 0, 2).reshape(chips, 2, -1, part)

    def reduce_mp(parts, extra):
        count, kind = parts.shape[2], parts.dtype
        theirs = lax.dynamic_index_in_dim(parts, 1 - core, 1, False)
        theirs = jnp.concatenate([theirs.reshape(chips * count, part), *extra], axis=0)
        theirs = swap_cores(theirs, mp_count).astype(jnp.float32)
        parts = lax.dynamic_index_in_dim(parts, core, 1, False).astype(jnp.float32)
        parts = parts + theirs[: chips * count].reshape(parts.shape)
        extra = [rows + theirs[chips * count :] for rows in extra]
        total = lax.dynamic_index_in_dim(parts, chip, 0, False)
        parts = parts.astype(kind)
        total = jnp.concatenate([total, *extra], axis=0)
        for step in range(1, chips):
            piece = lax.dynamic_index_in_dim(parts, (chip + step) % chips, 0, False)
            piece = shift_chips(jnp.concatenate([piece, *extra], axis=0), step)
            total = total + piece.astype(jnp.float32)
        return total

    state = state.astype(half)
    state_column = spread(state, "rows", column, by_z)
    states = [state_column]
    for step in range(1, line):
        pairs = [(i, i // line * line + (i - step) % line) for i in range(rows_count)]
        states.append(lax.ppermute(state_column, "rows", pairs))

    extra = jnp.pad(squares[None, :], ((0, 7), (0, part - docs)))
    gram = reduce_mp(by_part(contract_last(old_mine, old_all)), [extra])
    gram = jnp.concatenate([*halves(gram[:docs]), norm_rows(gram[docs, :docs], part)], axis=0)
    arrived = spread(gram, "rows", rows_count)
    gram = arrived[:, : 2 * docs]
    squares = arrived[:, 2 * docs].astype(jnp.float32)
    squares = squares[:, :docs] + squares[:, docs : 2 * docs]
    scale_rows = lax.rsqrt(squares / width + 1e-06).reshape(anchors, 1)

    count = slab.shape[0]
    slab_part = by_part(contract_last(slab, old_all).astype(half))
    slab_dual = reduce_mp(slab_part, []).astype(half)
    capacity = 2 * count // rows_count
    owner_ids = owners[:, 0]
    onehot = (owner_ids[:, None] == jnp.arange(rows_count, dtype=jnp.int32)[None, :]).astype(
        jnp.int32
    )
    counted = jnp.cumsum(onehot, axis=0)
    slot = jnp.sum((counted - 1) * onehot, axis=-1)
    target = owner_ids * capacity + slot
    routed = jnp.zeros((rows_count * capacity, part), half).at[target].set(slab_dual)
    routed, _ = lax.optimization_barrier((routed, arrived))
    routed = lax.all_to_all(routed.reshape(rows_count, capacity, part), "rows", 0, 0, tiled=True)

    grams = ring(gram, "mp", chips, mp_count, 2)
    grams = grams + [swap_cores(piece, mp_count) for piece in grams]
    routed_own = spread(routed, "mp", chips, by_y)
    routed_other = swap_cores(routed_own, mp_count)

    zero = jnp.zeros_like(core)
    here = jnp.stack([core, chip, lax.axis_index("rows") % line, zero]).astype(jnp.int32)
    dual_map = solve(
        here, scale_rows, my_cols(final_gain, 0).reshape(1, cols), *states, *grams
    )
    return apply_map(here, routed_own, routed_other, dual_map)


def solution(mesh):
    return jax.shard_map(
        local,
        mesh=mesh,
        in_specs=(
            P("rows", None),
            P(),
            P(None, "mp"),
            P(None, "mp"),
            P(None, "mp"),
            P("mp", None),
            P(),
            P(),
            P("rows", None, "mp"),
            P("rows", None, "mp"),
            P("rows"),
            P(),
            P("rows", None),
            P("rows", "mp"),
            P("rows", None),
        ),
        out_specs=P("rows", "mp"),
        check_vma=False,
    )
```

```python
import math

import jax
import jax.numpy as jnp
from jax import lax
from jax.experimental import pallas as pl
from jax.experimental.pallas import tpu as pltpu
from jax.sharding import PartitionSpec as P


D = 4096
HEADS = 32
KV_HEADS = 8
HEAD = 128
ITERS = 3


def rotate(values, position):
    half_width = values.shape[-1] // 2
    exponent = 2.0 * jnp.arange(half_width, dtype=jnp.float32) / values.shape[-1]
    frequency = jnp.exp(-exponent * math.log(1000000.0))
    angle = position[:, None, None] * frequency[None, None, :]
    cosine = jnp.cos(angle)
    sine = jnp.sin(angle)
    first = values[..., :half_width]
    second = values[..., half_width:]
    return jnp.concatenate(
        [first * cosine - second * sine, second * cosine + first * sine], axis=-1
    )


def head_norm(values, gain):
    scale = lax.rsqrt(jnp.mean(values * values, axis=-1, keepdims=True) + 1e-06)
    return values * scale * gain


TILE = 256
SMEM = pl.BlockSpec(memory_space=pltpu.SMEM)
VMEM = pl.BlockSpec(memory_space=pltpu.VMEM)
ANY = pl.BlockSpec(memory_space=pl.ANY)


def spread(block, axis, count, groups=None):
    copies = jnp.broadcast_to(block[None], (count,) + block.shape)
    return lax.all_to_all(copies, axis, 0, 0, tiled=True, axis_index_groups=groups)


def ring(block, axis, count, size, stride):
    def move(array, step):
        pairs = []
        for i in range(size):
            at = i // stride % count
            pairs.append((i, i + ((at + step) % count - at) * stride))
        return lax.ppermute(array, axis, pairs)

    below, above = [block, move(block, 1)], [block, move(block, -1)]
    middle = block.shape[0] // 2
    far = [move(below[-1][:middle], 1), move(above[-1][middle:], -1)]
    return above + below[:0:-1] + far


def swap_cores(block, size):
    return lax.ppermute(block, "mp", [(i, i ^ 1) for i in range(size)])


def tiles(body, init=0):
    return lax.fori_loop(0, 1024 // TILE, body, init)


def columns(place):
    return pl.ds(pl.multiple_of(place * 128, 128), 128)


def copy_all(pairs, sems):
    copies = [pltpu.make_async_copy(a, b, sems.at[i]) for i, (a, b) in enumerate(pairs)]
    for copy in copies:
        copy.start()
    return copies


def flat_dot(left, right):
    return lax.dot_general(
        left, right, (((1,), (1,)), ((), ())), preferred_element_type=jnp.float32
    )


def both(value):
    high = value.astype(jnp.bfloat16)
    return high, (value - high.astype(jnp.float32)).astype(jnp.bfloat16)


def norm_block(value):
    high = value.astype(jnp.bfloat16).astype(jnp.float32)
    row = lax.broadcasted_iota(jnp.int32, (16, value.shape[1]), 0)
    block = jnp.where(row == 0, high, jnp.where(row == 1, value - high, 0.0))
    return block.astype(jnp.bfloat16)


def fill(target, slab, gram, norms):
    target[:512] = slab.astype(jnp.bfloat16)
    target[512:544], target[544:576] = both(gram)
    target[576:592] = norms


def parts_kernel(here, slab, old_mine, old_all, squares, theirs, kept):
    norms = norm_block(squares[...])
    for y in range(4):
        for side in range(2):
            at = 2 * y + (here[0] if side else 1 - here[0])
            block = old_all[pl.ds(pl.multiple_of(at * 128, 128), 128), :]
            slab_part, gram_part = flat_dot(slab[...], block), flat_dot(old_mine[...], block)
            if side:
                kept[y, :512] = slab_part
                kept[y, 512:] = gram_part
            else:
                fill(theirs.at[y], slab_part, gram_part, norms)


def wide_sum(block):
    value = block.astype(jnp.float32)
    return value[:512], value[512:544] + value[544:576]


def pair_kernel(here, kept, theirs, squares, mine, total_squares, *pieces):
    total = squares[...] + jnp.sum(theirs[0, 576:].astype(jnp.float32), axis=0, keepdims=True)
    total_squares[...] = total
    norms = norm_block(total)
    for step in range(4):
        at = lax.rem(here[1] + step, 4)
        slab_part, gram_part = wide_sum(theirs[at])
        slab_part = kept[at, :512] + slab_part
        gram_part = kept[at, 512:] + gram_part
        if step:
            fill(pieces[step - 1], slab_part, gram_part, norms)
        else:
            mine[:512] = slab_part
            mine[512:] = gram_part


def route_kernel(target, mine, squares, *refs):
    pieces, outgoing = refs[:3], refs[3]
    slab_part, gram_part, total = mine[:512], mine[512:], squares[...]
    for piece in pieces:
        more_slab, more_gram = wide_sum(piece[...])
        slab_part, gram_part = slab_part + more_slab, gram_part + more_gram
        total = total + jnp.sum(piece[576:].astype(jnp.float32), axis=0, keepdims=True)
    slab_part = slab_part.astype(jnp.bfloat16)
    for tile in range(4):
        row = lax.broadcasted_iota(jnp.int32, (256, 512), 0) + 256 * tile
        chosen = jnp.where(row == target[...], 1.0, 0.0).astype(jnp.bfloat16)
        block = jnp.dot(chosen, slab_part, preferred_element_type=jnp.float32)
        outgoing[8 * tile : 8 * tile + 8, :32] = block.astype(jnp.bfloat16).reshape(8, 32, 128)
    high, low = both(gram_part)
    norms = norm_block(total)
    for owner in range(32):
        outgoing[owner, 32:64] = high
        outgoing[owner, 64:96] = low
        outgoing[owner, 96:112] = norms


def join_kernel(here, *refs):
    pieces, state = refs[:4], refs[4]
    for step, piece in enumerate(pieces):
        at = lax.rem(here[2] + step, 4)
        for z in range(8):
            state[z, at] = piece[z]


def solve_kernel(here, scale, gain, *refs):
    source, grams, slabs, result = refs[0], refs[1:11], refs[11:13], refs[13]
    state, high, low, rho, rho_high, rho_low, image, way, way_image, total = refs[14:24]
    routed, dual_map, state_sems, gram_sems, slab_sems = refs[24:]
    ridge = 0.125 * D
    state_copies = copy_all([(source, state)], state_sems)
    placed = []
    for index, piece in enumerate(grams):
        step, row = ((0, 0), (1, 0), (3, 0), (2, 0), (2, 16))[index % 5]
        side = here[0] if index < 5 else 1 - here[0]
        at = columns(2 * lax.rem(here[1] + step, 4) + side)
        docs = piece.shape[1] // 2
        rows = slice(row, row + piece.shape[0])
        placed.append((piece.at[:, :docs], high.at[rows, :, at]))
        placed.append((piece.at[:, docs:], low.at[rows, :, at]))
    gram_copies = copy_all(placed, gram_sems)
    placed = []
    for y in range(4):
        for side, piece in enumerate(slabs):
            at = 2 * y + (1 - here[0] if side else here[0])
            placed.append((piece.at[y], routed.at[:, :, columns(at)]))
    slab_copies = copy_all(placed, slab_sems)
    for copy in state_copies:
        copy.wait()

    def rows_of(i):
        return pl.ds(pl.multiple_of(i * TILE, TILE), TILE)

    def split(rows, value):
        rho[rows, :] = value
        top = value.astype(jnp.bfloat16)
        rho_high[rows, :] = top
        rho_low[rows, :] = (value - top.astype(jnp.float32)).astype(jnp.bfloat16)

    def start(i, carry):
        rows = rows_of(i)
        value = state[pl.ds(2 * i, 2)].reshape(TILE, -1).astype(jnp.float32)
        value = value * scale[rows, :] * gain[...]
        split(rows, value)
        way[rows, :] = value
        return carry

    tiles(start)
    for copy in gram_copies:
        copy.wait()

    def gram_rows(block, i):
        return block[pl.ds(8 * i, 8)].reshape(TILE, -1)

    def dot(left, right):
        return jnp.dot(left, right, preferred_element_type=jnp.float32)

    def product(i, square):
        rows = rows_of(i)
        top = gram_rows(high, i)
        value = dot(top, rho_low[...]) + dot(gram_rows(low, i), rho_high[...])
        value = value + dot(top, rho_high[...])
        image[rows, :] = value
        return square + jnp.sum(rho[rows, :] * value, axis=0, keepdims=True)

    zero = jnp.zeros((1, rho.shape[1]), jnp.float32)
    res_sq = tiles(product, zero)
    ratio = zero
    for sweep in range(ITERS):

        def turn(i, curvature):
            rows = rows_of(i)
            if sweep == 0:
                step, step_image = way[rows, :], image[rows, :]
            else:
                step = rho[rows, :] + ratio * way[rows, :]
                step_image = image[rows, :] + ratio * way_image[rows, :]
                way[rows, :] = step
            way_image[rows, :] = step_image
            return curvature + jnp.sum(
                step_image * (step_image + ridge * step), axis=0, keepdims=True
            )

        alpha = res_sq / tiles(turn, zero)

        def update(i, carry):
            rows = rows_of(i)
            step = way[rows, :]
            moved = alpha * step
            if sweep:
                moved = total[rows, :] + moved
            if sweep + 1 < ITERS:
                total[rows, :] = moved
                split(rows, rho[rows, :] - alpha * (way_image[rows, :] + ridge * step))
            else:
                dual_map[rows, :] = moved.astype(jnp.bfloat16)
            return carry

        tiles(update)
        if sweep + 1 < ITERS:
            new_sq = tiles(product, zero)
            ratio = new_sq / res_sq
            res_sq = new_sq

    for copy in slab_copies:
        copy.wait()

    def last(i, carry):
        result[rows_of(i), :] = dot(gram_rows(routed, i), dual_map[...]).astype(jnp.bfloat16)
        return carry

    tiles(last)


def call(kernel, shapes, in_specs, scratch, operands, flops, limit):
    return pl.pallas_call(
        kernel,
        out_shape=shapes,
        in_specs=in_specs,
        out_specs=jax.tree.map(lambda _: VMEM, shapes),
        scratch_shapes=scratch,
        cost_estimate=pl.CostEstimate(flops=flops, bytes_accessed=1 << 21, transcendentals=0),
        compiler_params=pltpu.CompilerParams(vmem_limit_bytes=limit << 20),
    )(*operands)


def join(*operands):
    shape = jax.ShapeDtypeStruct((8, 4) + operands[1].shape[1:], jnp.bfloat16)
    return call(join_kernel, shape, [SMEM] + [VMEM] * 4, [], operands, 1 << 20, 16)


def make_parts(*operands):
    shapes = (
        jax.ShapeDtypeStruct((4, 592, 128), jnp.bfloat16),
        jax.ShapeDtypeStruct((4, 544, 128), jnp.float32),
    )
    return call(parts_kernel, shapes, [SMEM] + [VMEM] * 4, [], operands, 1 << 30, 62)


def add_pair(*operands):
    shapes = (
        jax.ShapeDtypeStruct((544, 128), jnp.float32),
        jax.ShapeDtypeStruct((1, 128), jnp.float32),
    ) + (jax.ShapeDtypeStruct((592, 128), jnp.bfloat16),) * 3
    return call(pair_kernel, shapes, [SMEM] + [VMEM] * 3, [], operands, 1 << 20, 16)


def route(*operands):
    shape = jax.ShapeDtypeStruct((32, 112, 128), jnp.bfloat16)
    return call(route_kernel, shape, [VMEM] * 6, [], operands, 1 << 27, 16)


def solve(*operands):
    anchors, cols = operands[1].shape[0], operands[2].shape[1]
    wide = pltpu.VMEM((32, anchors // 32, anchors), jnp.bfloat16)
    full = pltpu.VMEM((anchors, cols), jnp.float32)
    half = pltpu.VMEM((anchors, cols), jnp.bfloat16)
    return call(
        solve_kernel,
        jax.ShapeDtypeStruct((anchors, cols), jnp.bfloat16),
        [SMEM, VMEM, VMEM] + [ANY] * 13,
        [pltpu.VMEM((8, 4, anchors // 32, cols), jnp.bfloat16), wide, wide, full, half, half]
        + [full] * 4
        + [wide, half]
        + [pltpu.SemaphoreType.DMA((count,)) for count in (1, 20, 8)],
        operands,
        18 * anchors * anchors * cols,
        62,
    )


def local(
    hidden,
    attn_gain,
    w_query,
    w_key,
    w_value,
    w_output,
    query_gain,
    key_gain,
    key_cache,
    value_cache,
    lengths,
    final_gain,
    old_embed,
    slab,
    owners,
):
    docs = hidden.shape[0]
    width = hidden.shape[1]
    kv_local = w_key.shape[1] // HEAD
    group = HEADS // KV_HEADS
    rows_count = lax.axis_size("rows")
    mp_count = lax.axis_size("mp")
    cols = width // mp_count
    hidden32 = hidden.astype(jnp.float32)
    normed = (
        hidden32
        * lax.rsqrt(jnp.mean(hidden32 * hidden32, axis=-1, keepdims=True) + 1e-06)
        * attn_gain
    ).astype(jnp.bfloat16)
    position = lengths.astype(jnp.float32)
    query = jnp.dot(normed, w_query, preferred_element_type=jnp.float32).reshape(
        docs, kv_local * group, HEAD
    )
    key_new = jnp.dot(normed, w_key, preferred_element_type=jnp.float32).reshape(
        docs, kv_local, HEAD
    )
    value_new = (
        jnp.dot(normed, w_value, preferred_element_type=jnp.float32)
        .reshape(docs, kv_local, HEAD)
        .astype(jnp.bfloat16)
    )
    query = rotate(head_norm(query, query_gain), position).astype(jnp.bfloat16)
    key_new = rotate(head_norm(key_new, key_gain), position).astype(jnp.bfloat16)
    query_groups = query.reshape(docs, kv_local, group, HEAD)
    keys = key_cache.reshape(docs, key_cache.shape[1], kv_local, HEAD)
    values = value_cache.reshape(docs, value_cache.shape[1], kv_local, HEAD)
    scale = 1.0 / math.sqrt(HEAD)
    scores = (
        jnp.einsum("akgd,apkd->akgp", query_groups, keys, preferred_element_type=jnp.float32)
        * scale
    )
    own_score = (
        jnp.einsum("akgd,akd->akg", query_groups, key_new, preferred_element_type=jnp.float32)
        * scale
    )
    valid = jnp.arange(keys.shape[1], dtype=jnp.int32)[None, :] < lengths[:, None]
    scores = jnp.where(valid[:, None, None, :], scores, -jnp.inf)
    top = jnp.maximum(jnp.max(scores, axis=-1), own_score)
    expo = jnp.exp(scores - top[..., None])
    own_expo = jnp.exp(own_score - top)
    total = jnp.sum(expo, axis=-1) + own_expo
    weights = (expo / total[..., None]).astype(jnp.bfloat16)
    own_weight = (own_expo / total).astype(jnp.bfloat16)
    attended = jnp.einsum("akgp,apkd->akgd", weights, values, preferred_element_type=jnp.float32)
    attended = (
        attended
        + own_weight.astype(jnp.float32)[..., None] * value_new.astype(jnp.float32)[:, :, None, :]
    )
    attended = attended.reshape(docs, kv_local * group * HEAD).astype(jnp.bfloat16)
    partial_value = lax.optimization_barrier(
        jnp.dot(attended, w_output, preferred_element_type=jnp.float32)
    )
    place_mp = lax.axis_index("mp")
    mine = place_mp * cols
    core, chip = place_mp % 2, place_mp // 2
    chips = mp_count // 2
    my_cols = lambda array, axis: lax.dynamic_slice_in_dim(array, mine, cols, axis)
    half = jnp.bfloat16

    def shift_chips(block, step):
        return lax.ppermute(
            block, "mp", [(i, (i + 2 * step) % mp_count) for i in range(mp_count)]
        )

    pieces = partial_value.reshape(docs, chips, 2, cols)
    theirs = lax.dynamic_index_in_dim(pieces, 1 - core, 2, False).astype(half)
    pieces = lax.dynamic_index_in_dim(pieces, core, 2, False)
    pieces = pieces + swap_cores(theirs, mp_count).astype(jnp.float32)
    state = my_cols(hidden32, 1) + lax.dynamic_index_in_dim(pieces, chip, 1, False)
    pieces = pieces.astype(half)
    for step in range(1, chips):
        piece = lax.dynamic_index_in_dim(pieces, (chip + step) % chips, 1, False)
        state = state + shift_chips(piece, step).astype(jnp.float32)
    squares = jnp.sum(state * state, axis=-1)

    line = 4
    column = rows_count // line
    by_z = [[x + line * z for z in range(column)] for x in range(line)]
    by_y = [list(range(at, mp_count, 2)) for at in range(2)]
    old_mine = my_cols(old_embed, 1)
    old_all = spread(old_mine, "rows", rows_count)
    anchors = rows_count * docs
    part = anchors // mp_count
    old_all = old_all.reshape(anchors, cols)

    state = state.astype(half)
    state_column = spread(state, "rows", column, by_z)
    states = [state_column]
    for step in range(1, line):
        pairs = [(i, i // line * line + (i - step) % line) for i in range(rows_count)]
        states.append(lax.ppermute(state_column, "rows", pairs))

    here = jnp.stack([core, chip, lax.axis_index("rows") % line, jnp.zeros_like(core)])
    here = here.astype(jnp.int32)
    state_all = join(here, *states)

    capacity = 2 * slab.shape[0] // rows_count
    owner_ids = owners[:, 0]
    onehot = (owner_ids[:, None] == jnp.arange(rows_count, dtype=jnp.int32)[None, :]).astype(
        jnp.int32
    )
    counted = jnp.cumsum(onehot, axis=0)
    slot = jnp.sum((counted - 1) * onehot, axis=-1)
    target = (owner_ids * capacity + slot).reshape(1, -1)

    squares = jnp.pad(squares[None, :], ((0, 0), (0, part - docs)))
    theirs, kept = make_parts(here, slab, old_mine, old_all, squares)
    theirs = swap_cores(theirs, mp_count)
    kept, squares, *pieces = add_pair(here, kept, theirs, squares)
    pieces = [shift_chips(piece, step) for step, piece in enumerate(pieces, 1)]
    outgoing = route(target, kept, squares, *pieces)
    arrived = lax.all_to_all(outgoing, "rows", 0, 0, tiled=True)
    routed = arrived[:, :capacity]
    gram = arrived[:, capacity : capacity + 2 * docs]
    squares = arrived[:, capacity + 2 * docs : capacity + 2 * docs + 2, :docs]
    squares = jnp.sum(squares.astype(jnp.float32), axis=1)
    scale_rows = lax.rsqrt(squares / width + 1e-06).reshape(anchors, 1)

    grams = ring(gram, "mp", chips, mp_count, 2)
    grams = grams + [swap_cores(piece, mp_count) for piece in grams]
    slabs = spread(routed, "mp", chips, by_y)
    slabs = [slabs, swap_cores(slabs, mp_count)]
    return solve(
        here, scale_rows, my_cols(final_gain, 0).reshape(1, cols), state_all, *grams, *slabs
    )


def solution(mesh):
    return jax.shard_map(
        local,
        mesh=mesh,
        in_specs=(
            P("rows", None),
            P(),
            P(None, "mp"),
            P(None, "mp"),
            P(None, "mp"),
            P("mp", None),
            P(),
            P(),
            P("rows", None, "mp"),
            P("rows", None, "mp"),
            P("rows"),
            P(),
            P("rows", None),
            P("rows", "mp"),
            P("rows", None),
        ),
        out_specs=P("rows", "mp"),
        check_vma=False,
    )
```

```python
import math

import jax
import jax.numpy as jnp
from jax import lax
from jax.experimental import pallas as pl
from jax.experimental.pallas import tpu as pltpu
from jax.sharding import PartitionSpec as P


D = 4096
HEADS = 32
KV_HEADS = 8
HEAD = 128
ITERS = 3


def rotate(values, position):
    half_width = values.shape[-1] // 2
    exponent = 2.0 * jnp.arange(half_width, dtype=jnp.float32) / values.shape[-1]
    frequency = jnp.exp(-exponent * math.log(1000000.0))
    angle = position[:, None, None] * frequency[None, None, :]
    cosine = jnp.cos(angle)
    sine = jnp.sin(angle)
    first = values[..., :half_width]
    second = values[..., half_width:]
    return jnp.concatenate(
        [first * cosine - second * sine, second * cosine + first * sine], axis=-1
    )


def head_norm(values, gain):
    scale = lax.rsqrt(jnp.mean(values * values, axis=-1, keepdims=True) + 1e-06)
    return values * scale * gain


TILE = 1024
STRIP = 32
SMEM = pl.BlockSpec(memory_space=pltpu.SMEM)
VMEM = pl.BlockSpec(memory_space=pltpu.VMEM)
ANY = pl.BlockSpec(memory_space=pl.ANY)


def spread(block, axis, count, groups=None):
    copies = jnp.broadcast_to(block[None], (count,) + block.shape)
    return lax.all_to_all(copies, axis, 0, 0, tiled=True, axis_index_groups=groups)


def ring(block, axis, count, size, stride):
    def move(array, step):
        pairs = []
        for i in range(size):
            at = i // stride % count
            pairs.append((i, i + ((at + step) % count - at) * stride))
        return lax.ppermute(array, axis, pairs)

    below, above = [block, move(block, 1)], [block, move(block, -1)]
    middle = block.shape[0] // 2
    far = [move(below[-1][:middle], 1), move(above[-1][middle:], -1)]
    return above + below[:0:-1] + far


def swap_cores(block, size):
    return lax.ppermute(block, "mp", [(i, i ^ 1) for i in range(size)])


def tiles(body, init=0):
    return lax.fori_loop(0, 1024 // TILE, body, init)


def strips(body, init=0):
    return lax.fori_loop(0, 1024 // STRIP, body, init, unroll=4)


def columns(place):
    return pl.ds(pl.multiple_of(place * 128, 128), 128)


def copy_all(pairs, sems):
    copies = [pltpu.make_async_copy(a, b, sems.at[i]) for i, (a, b) in enumerate(pairs)]
    for copy in copies:
        copy.start()
    return copies


def flat_dot(left, right):
    return lax.dot_general(
        left, right, (((1,), (1,)), ((), ())), preferred_element_type=jnp.float32
    )


def both(value):
    high = value.astype(jnp.bfloat16)
    return high, (value - high.astype(jnp.float32)).astype(jnp.bfloat16)


def norm_block(value):
    high = value.astype(jnp.bfloat16).astype(jnp.float32)
    row = lax.broadcasted_iota(jnp.int32, (16, value.shape[1]), 0)
    block = jnp.where(row == 0, high, jnp.where(row == 1, value - high, 0.0))
    return block.astype(jnp.bfloat16)


def fill(target, slab, gram, norms):
    target[:512] = slab.astype(jnp.bfloat16)
    target[512:544], target[544:576] = both(gram)
    target[576:592] = norms


def parts_kernel(here, slab, old_mine, old_all, squares, theirs, kept):
    norms = norm_block(squares[...])
    first = here[0] == 0
    for y in range(4):
        block = old_all[256 * y : 256 * (y + 1), :]
        slab_part, gram_part = flat_dot(slab[...], block), flat_dot(old_mine[...], block)
        left, right = slab_part[:, :128], slab_part[:, 128:]
        low, high = gram_part[:, :128], gram_part[:, 128:]
        kept[y, :512] = jnp.where(first, left, right)
        kept[y, 512:] = jnp.where(first, low, high)
        fill(
            theirs.at[y], jnp.where(first, right, left), jnp.where(first, high, low), norms
        )


def wide_sum(block):
    value = block.astype(jnp.float32)
    return value[:512], value[512:544] + value[544:576]


def pair_kernel(here, kept, theirs, squares, mine, total_squares, *pieces):
    total = squares[...] + jnp.sum(theirs[0, 576:].astype(jnp.float32), axis=0, keepdims=True)
    total_squares[...] = total
    norms = norm_block(total)
    for step in range(4):
        at = lax.rem(here[1] + step, 4)
        slab_part, gram_part = wide_sum(theirs[at])
        slab_part = kept[at, :512] + slab_part
        gram_part = kept[at, 512:] + gram_part
        if step:
            fill(pieces[step - 1], slab_part, gram_part, norms)
        else:
            mine[:512] = slab_part
            mine[512:] = gram_part


def route_kernel(target, mine, squares, *refs):
    pieces, outgoing = refs[:3], refs[3]
    slab_part, gram_part, total = mine[:512], mine[512:], squares[...]
    for piece in pieces:
        more_slab, more_gram = wide_sum(piece[...])
        slab_part, gram_part = slab_part + more_slab, gram_part + more_gram
        total = total + jnp.sum(piece[576:].astype(jnp.float32), axis=0, keepdims=True)
    slab_part = slab_part.astype(jnp.bfloat16)
    for tile in range(4):
        row = lax.broadcasted_iota(jnp.int32, (256, 512), 0) + 256 * tile
        chosen = jnp.where(row == target[...], 1.0, 0.0).astype(jnp.bfloat16)
        block = jnp.dot(chosen, slab_part, preferred_element_type=jnp.float32)
        outgoing[8 * tile : 8 * tile + 8, :32] = block.astype(jnp.bfloat16).reshape(8, 32, 128)
    high, low = both(gram_part)
    norms = norm_block(total)
    for owner in range(32):
        outgoing[owner, 32:64] = high
        outgoing[owner, 64:96] = low
        outgoing[owner, 96:112] = norms


def join_kernel(here, *refs):
    pieces, state = refs[:4], refs[4]
    for step, piece in enumerate(pieces):
        at = lax.rem(here[2] + step, 4)
        for z in range(8):
            state[z, at] = piece[z]


def solve_kernel(here, scale, gain, *refs):
    source, grams, slabs, result = refs[0], refs[1:11], refs[11:13], refs[13]
    state, high, low, rho, rho_high, rho_low, image, way, way_image, total = refs[14:24]
    routed, dual_map, state_sems, gram_sems, slab_sems = refs[24:]
    ridge = 0.125 * D
    state_copies = copy_all([(source, state)], state_sems)
    placed = []
    for index, piece in enumerate(grams):
        step, row = ((0, 0), (1, 0), (3, 0), (2, 0), (2, 16))[index % 5]
        side = here[0] if index < 5 else 1 - here[0]
        at = columns(2 * lax.rem(here[1] + step, 4) + side)
        docs = piece.shape[1] // 2
        rows = slice(row, row + piece.shape[0])
        placed.append((piece.at[:, :docs], high.at[rows, :, at]))
        placed.append((piece.at[:, docs:], low.at[rows, :, at]))
    gram_copies = copy_all(placed, gram_sems)
    placed = []
    for y in range(4):
        for side, piece in enumerate(slabs):
            at = 2 * y + (1 - here[0] if side else here[0])
            placed.append((piece.at[y], routed.at[:, :, columns(at)]))
    slab_copies = copy_all(placed, slab_sems)
    for copy in state_copies:
        copy.wait()

    def rows_of(i, size=STRIP):
        return pl.ds(pl.multiple_of(i * size, size), size)

    def split(rows, value):
        rho[rows, :] = value
        top = value.astype(jnp.bfloat16)
        rho_high[rows, :] = top
        rho_low[rows, :] = (value - top.astype(jnp.float32)).astype(jnp.bfloat16)

    def start(i, carry):
        rows = rows_of(i)
        value = state[i // 4, i % 4].astype(jnp.float32)
        value = (value * scale[rows, :] * gain[...]).astype(jnp.bfloat16)
        rho_high[rows, :] = value
        rho[rows, :] = value.astype(jnp.float32)
        return carry

    strips(start)
    for copy in gram_copies:
        copy.wait()

    def gram_rows(block, i):
        return block[pl.ds(TILE // 32 * i, TILE // 32)].reshape(TILE, -1)

    def dot(left, right):
        return jnp.dot(left, right, preferred_element_type=jnp.float32)

    def product(i, sums, exact=False):
        rows = rows_of(i, TILE)
        top = gram_rows(high, i)
        value = dot(gram_rows(low, i), rho_high[...])
        if not exact:
            value = value + dot(top, rho_low[...])
        value = value + dot(top, rho_high[...])
        image[rows, :] = value
        here_rho = rho[rows, :]
        square, bend = sums
        return (
            square + jnp.sum(here_rho * value, axis=0, keepdims=True),
            bend + jnp.sum(value * (value + ridge * here_rho), axis=0, keepdims=True),
        )

    zero = jnp.zeros((1, rho.shape[1]), jnp.float32)
    res_sq, curvature = tiles(lambda i, sums: product(i, sums, True), (zero, zero))
    for sweep in range(ITERS):
        if sweep:

            def turn(i, bend):
                rows = rows_of(i)
                step = rho[rows, :] + ratio * way[rows, :]
                step_image = image[rows, :] + ratio * way_image[rows, :]
                way[rows, :] = step
                way_image[rows, :] = step_image
                return bend + jnp.sum(
                    step_image * (step_image + ridge * step), axis=0, keepdims=True
                )

            curvature = strips(turn, zero)
        alpha = res_sq / curvature

        def update(i, carry):
            rows = rows_of(i)
            if sweep:
                step, step_image = way[rows, :], way_image[rows, :]
                moved = total[rows, :] + alpha * step
            else:
                step, step_image = rho[rows, :], image[rows, :]
                way[rows, :] = step
                way_image[rows, :] = step_image
                moved = alpha * step
            if sweep + 1 < ITERS:
                total[rows, :] = moved
                split(rows, rho[rows, :] - alpha * (step_image + ridge * step))
            else:
                dual_map[rows, :] = moved.astype(jnp.bfloat16)
            return carry

        strips(update)
        if sweep + 1 < ITERS:
            new_sq, _ = tiles(product, (zero, zero))
            ratio = new_sq / res_sq
            res_sq = new_sq

    for copy in slab_copies:
        copy.wait()

    def last(i, carry):
        result[rows_of(i, TILE), :] = dot(gram_rows(routed, i), dual_map[...]).astype(jnp.bfloat16)
        return carry

    tiles(last)


def call(kernel, shapes, in_specs, scratch, operands, flops, limit):
    return pl.pallas_call(
        kernel,
        out_shape=shapes,
        in_specs=in_specs,
        out_specs=jax.tree.map(lambda _: VMEM, shapes),
        scratch_shapes=scratch,
        cost_estimate=pl.CostEstimate(flops=flops, bytes_accessed=1 << 21, transcendentals=0),
        compiler_params=pltpu.CompilerParams(vmem_limit_bytes=limit << 20),
    )(*operands)


def join(*operands):
    shape = jax.ShapeDtypeStruct((8, 4) + operands[1].shape[1:], jnp.bfloat16)
    return call(join_kernel, shape, [SMEM] + [VMEM] * 4, [], operands, 1 << 20, 16)


def make_parts(*operands):
    shapes = (
        jax.ShapeDtypeStruct((4, 592, 128), jnp.bfloat16),
        jax.ShapeDtypeStruct((4, 544, 128), jnp.float32),
    )
    return call(parts_kernel, shapes, [SMEM] + [VMEM] * 4, [], operands, 1 << 30, 62)


def add_pair(*operands):
    shapes = (
        jax.ShapeDtypeStruct((544, 128), jnp.float32),
        jax.ShapeDtypeStruct((1, 128), jnp.float32),
    ) + (jax.ShapeDtypeStruct((592, 128), jnp.bfloat16),) * 3
    return call(pair_kernel, shapes, [SMEM] + [VMEM] * 3, [], operands, 1 << 20, 16)


def route(*operands):
    shape = jax.ShapeDtypeStruct((32, 112, 128), jnp.bfloat16)
    return call(route_kernel, shape, [VMEM] * 6, [], operands, 1 << 27, 16)


def solve(*operands):
    anchors, cols = operands[1].shape[0], operands[2].shape[1]
    wide = pltpu.VMEM((32, anchors // 32, anchors), jnp.bfloat16)
    full = pltpu.VMEM((anchors, cols), jnp.float32)
    half = pltpu.VMEM((anchors, cols), jnp.bfloat16)
    return call(
        solve_kernel,
        jax.ShapeDtypeStruct((anchors, cols), jnp.bfloat16),
        [SMEM, VMEM, VMEM] + [ANY] * 13,
        [pltpu.VMEM((8, 4, anchors // 32, cols), jnp.bfloat16), wide, wide, full, half, half]
        + [full] * 4
        + [wide, half]
        + [pltpu.SemaphoreType.DMA((count,)) for count in (1, 20, 8)],
        operands,
        18 * anchors * anchors * cols,
        62,
    )


def local(
    hidden,
    attn_gain,
    w_query,
    w_key,
    w_value,
    w_output,
    query_gain,
    key_gain,
    key_cache,
    value_cache,
    lengths,
    final_gain,
    old_embed,
    slab,
    owners,
):
    docs = hidden.shape[0]
    width = hidden.shape[1]
    kv_local = w_key.shape[1] // HEAD
    group = HEADS // KV_HEADS
    rows_count = lax.axis_size("rows")
    mp_count = lax.axis_size("mp")
    cols = width // mp_count
    hidden32 = hidden.astype(jnp.float32)
    normed = (
        hidden32
        * lax.rsqrt(jnp.mean(hidden32 * hidden32, axis=-1, keepdims=True) + 1e-06)
        * attn_gain
    ).astype(jnp.bfloat16)
    position = lengths.astype(jnp.float32)
    query = jnp.dot(normed, w_query, preferred_element_type=jnp.float32).reshape(
        docs, kv_local * group, HEAD
    )
    key_new = jnp.dot(normed, w_key, preferred_element_type=jnp.float32).reshape(
        docs, kv_local, HEAD
    )
    value_new = (
        jnp.dot(normed, w_value, preferred_element_type=jnp.float32)
        .reshape(docs, kv_local, HEAD)
        .astype(jnp.bfloat16)
    )
    query = rotate(head_norm(query, query_gain), position).astype(jnp.bfloat16)
    key_new = rotate(head_norm(key_new, key_gain), position).astype(jnp.bfloat16)
    query_groups = query.reshape(docs, kv_local, group, HEAD)
    keys = key_cache.reshape(docs, key_cache.shape[1], kv_local, HEAD)
    values = value_cache.reshape(docs, value_cache.shape[1], kv_local, HEAD)
    scale = 1.0 / math.sqrt(HEAD)
    scores = (
        jnp.einsum("akgd,apkd->akgp", query_groups, keys, preferred_element_type=jnp.float32)
        * scale
    )
    own_score = (
        jnp.einsum("akgd,akd->akg", query_groups, key_new, preferred_element_type=jnp.float32)
        * scale
    )
    valid = jnp.arange(keys.shape[1], dtype=jnp.int32)[None, :] < lengths[:, None]
    scores = jnp.where(valid[:, None, None, :], scores, -jnp.inf)
    top = jnp.maximum(jnp.max(scores, axis=-1), own_score)
    expo = jnp.exp(scores - top[..., None])
    own_expo = jnp.exp(own_score - top)
    total = jnp.sum(expo, axis=-1) + own_expo
    weights = (expo / total[..., None]).astype(jnp.bfloat16)
    own_weight = (own_expo / total).astype(jnp.bfloat16)
    attended = jnp.einsum("akgp,apkd->akgd", weights, values, preferred_element_type=jnp.float32)
    attended = (
        attended
        + own_weight.astype(jnp.float32)[..., None] * value_new.astype(jnp.float32)[:, :, None, :]
    )
    attended = attended.reshape(docs, kv_local * group * HEAD).astype(jnp.bfloat16)
    partial_value = lax.optimization_barrier(
        jnp.dot(attended, w_output, preferred_element_type=jnp.float32)
    )
    place_mp = lax.axis_index("mp")
    mine = place_mp * cols
    core, chip = place_mp % 2, place_mp // 2
    chips = mp_count // 2
    my_cols = lambda array, axis: lax.dynamic_slice_in_dim(array, mine, cols, axis)
    half = jnp.bfloat16

    def shift_chips(block, step):
        return lax.ppermute(
            block, "mp", [(i, (i + 2 * step) % mp_count) for i in range(mp_count)]
        )

    pieces = partial_value.reshape(docs, chips, 2, cols)
    theirs = lax.dynamic_index_in_dim(pieces, 1 - core, 2, False).astype(half)
    pieces = lax.dynamic_index_in_dim(pieces, core, 2, False)
    pieces = pieces + swap_cores(theirs, mp_count).astype(jnp.float32)
    state = my_cols(hidden32, 1) + lax.dynamic_index_in_dim(pieces, chip, 1, False)
    pieces = pieces.astype(half)
    for step in range(1, chips):
        piece = lax.dynamic_index_in_dim(pieces, (chip + step) % chips, 1, False)
        state = state + shift_chips(piece, step).astype(jnp.float32)
    squares = jnp.sum(state * state, axis=-1)

    line = 4
    column = rows_count // line
    by_z = [[x + line * z for z in range(column)] for x in range(line)]
    by_y = [list(range(at, mp_count, 2)) for at in range(2)]
    gain = my_cols(final_gain, 0).reshape(1, cols)
    old_mine = my_cols(old_embed, 1)
    old_all = spread(old_mine, "rows", rows_count)
    anchors = rows_count * docs
    part = anchors // mp_count
    old_all = old_all.reshape(anchors, cols)

    state = state.astype(half)
    state_column = spread(state, "rows", column, by_z)
    states = [state_column]
    for step in range(1, line):
        pairs = [(i, i // line * line + (i - step) % line) for i in range(rows_count)]
        states.append(lax.ppermute(state_column, "rows", pairs))

    here = jnp.stack([core, chip, lax.axis_index("rows") % line, jnp.zeros_like(core)])
    here = here.astype(jnp.int32)
    state_all = join(here, *states)

    capacity = 2 * slab.shape[0] // rows_count
    owner_ids = owners[:, 0]
    onehot = (owner_ids[:, None] == jnp.arange(rows_count, dtype=jnp.int32)[None, :]).astype(
        jnp.int32
    )
    counted = jnp.cumsum(onehot, axis=0)
    slot = jnp.sum((counted - 1) * onehot, axis=-1)
    target = (owner_ids * capacity + slot).reshape(1, -1)

    squares = jnp.pad(squares[None, :], ((0, 0), (0, part - docs)))
    theirs, kept = make_parts(here, slab, old_mine, old_all, squares)
    theirs = swap_cores(theirs, mp_count)
    kept, squares, *pieces = add_pair(here, kept, theirs, squares)
    pieces = [shift_chips(piece, step) for step, piece in enumerate(pieces, 1)]
    outgoing = route(target, kept, squares, *pieces)
    arrived = lax.all_to_all(outgoing, "rows", 0, 0, tiled=True)
    routed = arrived[:, :capacity]
    gram = arrived[:, capacity : capacity + 2 * docs]
    squares = arrived[:, capacity + 2 * docs : capacity + 2 * docs + 2, :docs]
    squares = jnp.sum(squares.astype(jnp.float32), axis=1)
    scale_rows = lax.rsqrt(squares / width + 1e-06).reshape(anchors, 1)

    grams = ring(gram, "mp", chips, mp_count, 2)
    grams = grams + [swap_cores(piece, mp_count) for piece in grams]
    slabs = spread(routed, "mp", chips, by_y)
    slabs = [slabs, swap_cores(slabs, mp_count)]
    return solve(
        here, scale_rows, gain, state_all, *grams, *slabs
    )


def solution(mesh):
    return jax.shard_map(
        local,
        mesh=mesh,
        in_specs=(
            P("rows", None),
            P(),
            P(None, "mp"),
            P(None, "mp"),
            P(None, "mp"),
            P("mp", None),
            P(),
            P(),
            P("rows", None, "mp"),
            P("rows", None, "mp"),
            P("rows"),
            P(),
            P("rows", None),
            P("rows", "mp"),
            P("rows", None),
        ),
        out_specs=P("rows", "mp"),
        check_vma=False,
    )
```

```python
import math

import jax
import jax.numpy as jnp
from jax import lax
from jax.experimental import pallas as pl
from jax.experimental.pallas import tpu as pltpu
from jax.sharding import PartitionSpec as P


D = 4096
HEADS = 32
KV_HEADS = 8
HEAD = 128
ITERS = 3


def rotate(values, position):
    half_width = values.shape[-1] // 2
    exponent = 2.0 * jnp.arange(half_width, dtype=jnp.float32) / values.shape[-1]
    frequency = jnp.exp(-exponent * math.log(1000000.0))
    angle = position[:, None, None] * frequency[None, None, :]
    cosine = jnp.cos(angle)
    sine = jnp.sin(angle)
    first = values[..., :half_width]
    second = values[..., half_width:]
    return jnp.concatenate(
        [first * cosine - second * sine, second * cosine + first * sine], axis=-1
    )


def head_norm(values, gain):
    scale = lax.rsqrt(jnp.mean(values * values, axis=-1, keepdims=True) + 1e-06)
    return values * scale * gain


TILE = 1024
STRIP = 32
SMEM = pl.BlockSpec(memory_space=pltpu.SMEM)
VMEM = pl.BlockSpec(memory_space=pltpu.VMEM)
ANY = pl.BlockSpec(memory_space=pl.ANY)


def spread(block, axis, count, groups=None):
    copies = jnp.broadcast_to(block[None], (count,) + block.shape)
    return lax.all_to_all(copies, axis, 0, 0, tiled=True, axis_index_groups=groups)


def ring(block, axis, count, size, stride):
    def move(array, step):
        pairs = []
        for i in range(size):
            at = i // stride % count
            pairs.append((i, i + ((at + step) % count - at) * stride))
        return lax.ppermute(array, axis, pairs)

    below, above = [block, move(block, 1)], [block, move(block, -1)]
    middle = block.shape[0] // 2
    far = [move(below[-1][:middle], 1), move(above[-1][middle:], -1)]
    return above + below[:0:-1] + far


def swap_cores(block, size):
    return lax.ppermute(block, "mp", [(i, i ^ 1) for i in range(size)])


def tiles(body, init=0):
    return lax.fori_loop(0, 1024 // TILE, body, init)


def strips(body, init=0):
    return lax.fori_loop(0, 1024 // STRIP, body, init, unroll=4)


def columns(place):
    return pl.ds(pl.multiple_of(place * 128, 128), 128)


def copy_all(pairs, sems):
    copies = [pltpu.make_async_copy(a, b, sems.at[i]) for i, (a, b) in enumerate(pairs)]
    for copy in copies:
        copy.start()
    return copies


def flat_dot(left, right):
    return lax.dot_general(
        left, right, (((1,), (1,)), ((), ())), preferred_element_type=jnp.float32
    )


def both(value):
    high = value.astype(jnp.bfloat16)
    return high, (value - high.astype(jnp.float32)).astype(jnp.bfloat16)


def norm_block(value):
    high = value.astype(jnp.bfloat16).astype(jnp.float32)
    row = lax.broadcasted_iota(jnp.int32, (8, value.shape[1]), 0)
    block = jnp.where(row == 0, high, jnp.where(row == 1, value - high, 0.0))
    return block.astype(jnp.bfloat16)


def fill(target, slab, gram, norms):
    target[:512] = slab.astype(jnp.bfloat16)
    target[512:544], target[544:576] = both(gram)
    target[576:584] = norms


def parts_kernel(here, slab, old_mine, old_all, squares, theirs, kept):
    norms = norm_block(squares[...])
    first = here[0] == 0
    for y in range(4):
        block = old_all[256 * y : 256 * (y + 1), :]
        slab_part, gram_part = flat_dot(slab[...], block), flat_dot(old_mine[...], block)
        left, right = slab_part[:, :128], slab_part[:, 128:]
        low, high = gram_part[:, :128], gram_part[:, 128:]
        kept[y, :512] = jnp.where(first, left, right)
        kept[y, 512:] = jnp.where(first, low, high)
        fill(
            theirs.at[y], jnp.where(first, right, left), jnp.where(first, high, low), norms
        )


def wide_sum(block):
    value = block.astype(jnp.float32)
    return value[:512], value[512:544] + value[544:576]


def pair_kernel(here, kept, theirs, squares, mine, total_squares, *pieces):
    total = squares[...] + jnp.sum(theirs[0, 576:].astype(jnp.float32), axis=0, keepdims=True)
    total_squares[...] = total
    norms = norm_block(total)
    for step in range(4):
        at = lax.rem(here[1] + step, 4)
        slab_part, gram_part = wide_sum(theirs[at])
        slab_part = kept[at, :512] + slab_part
        gram_part = kept[at, 512:] + gram_part
        if step:
            fill(pieces[step - 1], slab_part, gram_part, norms)
        else:
            mine[:512] = slab_part
            mine[512:] = gram_part


def route_kernel(target, mine, squares, *refs):
    pieces, outgoing = refs[:3], refs[3]
    slab_part, gram_part, total = mine[:512], mine[512:], squares[...]
    for piece in pieces:
        more_slab, more_gram = wide_sum(piece[...])
        slab_part, gram_part = slab_part + more_slab, gram_part + more_gram
        total = total + jnp.sum(piece[576:].astype(jnp.float32), axis=0, keepdims=True)
    slab_part = slab_part.astype(jnp.bfloat16)
    for tile in range(4):
        row = lax.broadcasted_iota(jnp.int32, (256, 512), 0) + 256 * tile
        chosen = jnp.where(row == target[...], 1.0, 0.0).astype(jnp.bfloat16)
        block = jnp.dot(chosen, slab_part, preferred_element_type=jnp.float32)
        outgoing[8 * tile : 8 * tile + 8, :32] = block.astype(jnp.bfloat16).reshape(8, 32, 128)
    high, low = both(gram_part)
    norms = norm_block(total)
    for owner in range(32):
        outgoing[owner, 32:64] = high
        outgoing[owner, 64:96] = low
        outgoing[owner, 96:104] = norms


def join_kernel(here, *refs):
    pieces, state = refs[:4], refs[4]
    for step, piece in enumerate(pieces):
        at = lax.rem(here[2] + step, 4)
        for z in range(8):
            state[z, at] = piece[z]


def solve_kernel(here, scale, gain, *refs):
    source, grams, slabs, result = refs[0], refs[1:11], refs[11:13], refs[13]
    state, high, low, rho, rho_high, rho_low, image, way, way_image, total = refs[14:24]
    routed, dual_map, state_sems, gram_sems, slab_sems = refs[24:]
    ridge = 0.125 * D
    state_copies = copy_all([(source, state)], state_sems)
    placed = []
    for index, piece in enumerate(grams):
        step, row = ((0, 0), (1, 0), (3, 0), (2, 0), (2, 16))[index % 5]
        side = here[0] if index < 5 else 1 - here[0]
        at = columns(2 * lax.rem(here[1] + step, 4) + side)
        docs = piece.shape[1] // 2
        rows = slice(row, row + piece.shape[0])
        placed.append((piece.at[:, :docs], high.at[rows, :, at]))
        placed.append((piece.at[:, docs:], low.at[rows, :, at]))
    gram_copies = copy_all(placed, gram_sems)
    placed = []
    for y in range(4):
        for side, piece in enumerate(slabs):
            at = 2 * y + (1 - here[0] if side else here[0])
            placed.append((piece.at[y], routed.at[:, :, columns(at)]))
    slab_copies = copy_all(placed, slab_sems)
    for copy in state_copies:
        copy.wait()

    def rows_of(i, size=STRIP):
        return pl.ds(pl.multiple_of(i * size, size), size)

    def split(rows, value):
        rho[rows, :] = value
        top = value.astype(jnp.bfloat16)
        rho_high[rows, :] = top
        rho_low[rows, :] = (value - top.astype(jnp.float32)).astype(jnp.bfloat16)

    def start(i, carry):
        rows = rows_of(i)
        value = state[i // 4, i % 4].astype(jnp.float32)
        value = (value * scale[rows, :] * gain[...]).astype(jnp.bfloat16)
        rho_high[rows, :] = value
        rho[rows, :] = value.astype(jnp.float32)
        return carry

    strips(start)
    for copy in gram_copies:
        copy.wait()

    def gram_rows(block, i):
        return block[pl.ds(TILE // 32 * i, TILE // 32)].reshape(TILE, -1)

    def dot(left, right):
        return jnp.dot(left, right, preferred_element_type=jnp.float32)

    def product(i, sums, exact=False):
        rows = rows_of(i, TILE)
        top = gram_rows(high, i)
        value = dot(gram_rows(low, i), rho_high[...])
        if not exact:
            value = value + dot(top, rho_low[...])
        value = value + dot(top, rho_high[...])
        image[rows, :] = value
        here_rho = rho[rows, :]
        square, bend = sums
        return (
            square + jnp.sum(here_rho * value, axis=0, keepdims=True),
            bend + jnp.sum(value * (value + ridge * here_rho), axis=0, keepdims=True),
        )

    zero = jnp.zeros((1, rho.shape[1]), jnp.float32)
    res_sq, curvature = tiles(lambda i, sums: product(i, sums, True), (zero, zero))
    for sweep in range(ITERS):
        if sweep:

            def turn(i, bend):
                rows = rows_of(i)
                step = rho[rows, :] + ratio * way[rows, :]
                step_image = image[rows, :] + ratio * way_image[rows, :]
                way[rows, :] = step
                way_image[rows, :] = step_image
                return bend + jnp.sum(
                    step_image * (step_image + ridge * step), axis=0, keepdims=True
                )

            curvature = strips(turn, zero)
        alpha = res_sq / curvature

        def update(i, carry):
            rows = rows_of(i)
            if sweep:
                step, step_image = way[rows, :], way_image[rows, :]
                moved = total[rows, :] + alpha * step
            else:
                step, step_image = rho[rows, :], image[rows, :]
                way[rows, :] = step
                way_image[rows, :] = step_image
                moved = alpha * step
            if sweep + 1 < ITERS:
                total[rows, :] = moved
                split(rows, rho[rows, :] - alpha * (step_image + ridge * step))
            else:
                dual_map[rows, :] = moved.astype(jnp.bfloat16)
            return carry

        strips(update)
        if sweep + 1 < ITERS:
            new_sq, _ = tiles(product, (zero, zero))
            ratio = new_sq / res_sq
            res_sq = new_sq

    for copy in slab_copies:
        copy.wait()

    def last(i, carry):
        result[rows_of(i, TILE), :] = dot(gram_rows(routed, i), dual_map[...]).astype(jnp.bfloat16)
        return carry

    tiles(last)


def call(kernel, shapes, in_specs, scratch, operands, flops, limit):
    return pl.pallas_call(
        kernel,
        out_shape=shapes,
        in_specs=in_specs,
        out_specs=jax.tree.map(lambda _: VMEM, shapes),
        scratch_shapes=scratch,
        cost_estimate=pl.CostEstimate(flops=flops, bytes_accessed=1 << 21, transcendentals=0),
        compiler_params=pltpu.CompilerParams(vmem_limit_bytes=limit << 20),
    )(*operands)


def unpack_kernel(arrived, gram, routed):
    gram[...] = arrived[:, 32:96]
    for chip in range(4):
        routed[chip] = arrived[:, :32]


def unpack(arrived):
    shapes = (
        jax.ShapeDtypeStruct((32, 64, 128), jnp.bfloat16),
        jax.ShapeDtypeStruct((4, 32, 32, 128), jnp.bfloat16),
    )
    return call(unpack_kernel, shapes, [VMEM], [], [arrived], 1 << 20, 62)


def join(*operands):
    shape = jax.ShapeDtypeStruct((8, 4) + operands[1].shape[1:], jnp.bfloat16)
    return call(join_kernel, shape, [SMEM] + [VMEM] * 4, [], operands, 1 << 20, 16)


def make_parts(*operands):
    shapes = (
        jax.ShapeDtypeStruct((4, 584, 128), jnp.bfloat16),
        jax.ShapeDtypeStruct((4, 544, 128), jnp.float32),
    )
    return call(parts_kernel, shapes, [SMEM] + [VMEM] * 4, [], operands, 1 << 30, 62)


def add_pair(*operands):
    shapes = (
        jax.ShapeDtypeStruct((544, 128), jnp.float32),
        jax.ShapeDtypeStruct((1, 128), jnp.float32),
    ) + (jax.ShapeDtypeStruct((584, 128), jnp.bfloat16),) * 3
    return call(pair_kernel, shapes, [SMEM] + [VMEM] * 3, [], operands, 1 << 20, 62)


def route(*operands):
    shape = jax.ShapeDtypeStruct((32, 104, 128), jnp.bfloat16)
    return call(route_kernel, shape, [VMEM] * 6, [], operands, 1 << 27, 62)


def solve(*operands):
    anchors, cols = operands[1].shape[0], operands[2].shape[1]
    wide = pltpu.VMEM((32, anchors // 32, anchors), jnp.bfloat16)
    full = pltpu.VMEM((anchors, cols), jnp.float32)
    half = pltpu.VMEM((anchors, cols), jnp.bfloat16)
    return call(
        solve_kernel,
        jax.ShapeDtypeStruct((anchors, cols), jnp.bfloat16),
        [SMEM, VMEM, VMEM] + [ANY] * 13,
        [pltpu.VMEM((8, 4, anchors // 32, cols), jnp.bfloat16), wide, wide, full, half, half]
        + [full] * 4
        + [wide, half]
        + [pltpu.SemaphoreType.DMA((count,)) for count in (1, 20, 8)],
        operands,
        18 * anchors * anchors * cols,
        62,
    )


def local(
    hidden,
    attn_gain,
    w_query,
    w_key,
    w_value,
    w_output,
    query_gain,
    key_gain,
    key_cache,
    value_cache,
    lengths,
    final_gain,
    old_embed,
    slab,
    owners,
):
    docs = hidden.shape[0]
    width = hidden.shape[1]
    kv_local = w_key.shape[1] // HEAD
    group = HEADS // KV_HEADS
    rows_count = lax.axis_size("rows")
    mp_count = lax.axis_size("mp")
    cols = width // mp_count
    hidden32 = hidden.astype(jnp.float32)
    normed = (
        hidden32
        * lax.rsqrt(jnp.mean(hidden32 * hidden32, axis=-1, keepdims=True) + 1e-06)
        * attn_gain
    ).astype(jnp.bfloat16)
    position = lengths.astype(jnp.float32)
    query = jnp.dot(normed, w_query, preferred_element_type=jnp.float32).reshape(
        docs, kv_local * group, HEAD
    )
    key_new = jnp.dot(normed, w_key, preferred_element_type=jnp.float32).reshape(
        docs, kv_local, HEAD
    )
    value_new = (
        jnp.dot(normed, w_value, preferred_element_type=jnp.float32)
        .reshape(docs, kv_local, HEAD)
        .astype(jnp.bfloat16)
    )
    query = rotate(head_norm(query, query_gain), position).astype(jnp.bfloat16)
    key_new = rotate(head_norm(key_new, key_gain), position).astype(jnp.bfloat16)
    query_groups = query.reshape(docs, kv_local, group, HEAD)
    keys = key_cache.reshape(docs, key_cache.shape[1], kv_local, HEAD)
    values = value_cache.reshape(docs, value_cache.shape[1], kv_local, HEAD)
    scale = 1.0 / math.sqrt(HEAD)
    scores = (
        jnp.einsum("akgd,apkd->akgp", query_groups, keys, preferred_element_type=jnp.float32)
        * scale
    )
    own_score = (
        jnp.einsum("akgd,akd->akg", query_groups, key_new, preferred_element_type=jnp.float32)
        * scale
    )
    valid = jnp.arange(keys.shape[1], dtype=jnp.int32)[None, :] < lengths[:, None]
    scores = jnp.where(valid[:, None, None, :], scores, -jnp.inf)
    top = jnp.maximum(jnp.max(scores, axis=-1), own_score)
    expo = jnp.exp(scores - top[..., None])
    own_expo = jnp.exp(own_score - top)
    total = jnp.sum(expo, axis=-1) + own_expo
    weights = (expo / total[..., None]).astype(jnp.bfloat16)
    own_weight = (own_expo / total).astype(jnp.bfloat16)
    attended = jnp.einsum("akgp,apkd->akgd", weights, values, preferred_element_type=jnp.float32)
    attended = (
        attended
        + own_weight.astype(jnp.float32)[..., None] * value_new.astype(jnp.float32)[:, :, None, :]
    )
    attended = attended.reshape(docs, kv_local * group * HEAD).astype(jnp.bfloat16)
    partial_value = lax.optimization_barrier(
        jnp.dot(attended, w_output, preferred_element_type=jnp.float32)
    )
    place_mp = lax.axis_index("mp")
    mine = place_mp * cols
    core, chip = place_mp % 2, place_mp // 2
    chips = mp_count // 2
    my_cols = lambda array, axis: lax.dynamic_slice_in_dim(array, mine, cols, axis)
    half = jnp.bfloat16

    def shift_chips(block, step):
        return lax.ppermute(
            block, "mp", [(i, (i + 2 * step) % mp_count) for i in range(mp_count)]
        )

    pieces = partial_value.reshape(docs, chips, 2, cols)
    theirs = lax.dynamic_index_in_dim(pieces, 1 - core, 2, False).astype(half)
    pieces = lax.dynamic_index_in_dim(pieces, core, 2, False)
    pieces = pieces + swap_cores(theirs, mp_count).astype(jnp.float32)
    state = my_cols(hidden32, 1) + lax.dynamic_index_in_dim(pieces, chip, 1, False)
    pieces = pieces.astype(half)
    for step in range(1, chips):
        piece = lax.dynamic_index_in_dim(pieces, (chip + step) % chips, 1, False)
        state = state + shift_chips(piece, step).astype(jnp.float32)
    squares = jnp.sum(state * state, axis=-1)

    line = 4
    column = rows_count // line
    by_z = [[x + line * z for z in range(column)] for x in range(line)]
    by_y = [list(range(at, mp_count, 2)) for at in range(2)]
    gain = my_cols(final_gain, 0).reshape(1, cols)
    old_mine = my_cols(old_embed, 1)
    old_all = spread(old_mine, "rows", rows_count)
    anchors = rows_count * docs
    part = anchors // mp_count
    old_all = old_all.reshape(anchors, cols)

    state = state.astype(half)
    state_column = spread(state, "rows", column, by_z)
    states = [state_column]
    for step in range(1, line):
        pairs = [(i, i // line * line + (i - step) % line) for i in range(rows_count)]
        states.append(lax.ppermute(state_column, "rows", pairs))

    here = jnp.stack([core, chip, lax.axis_index("rows") % line, jnp.zeros_like(core)])
    here = here.astype(jnp.int32)
    state_all = join(here, *states)

    capacity = 2 * slab.shape[0] // rows_count
    owner_ids = owners[:, 0]
    onehot = (owner_ids[:, None] == jnp.arange(rows_count, dtype=jnp.int32)[None, :]).astype(
        jnp.int32
    )
    counted = jnp.cumsum(onehot, axis=0)
    slot = jnp.sum((counted - 1) * onehot, axis=-1)
    target = (owner_ids * capacity + slot).reshape(1, -1)

    squares = jnp.pad(squares[None, :], ((0, 0), (0, part - docs)))
    theirs, kept = make_parts(here, slab, old_mine, old_all, squares)
    theirs = swap_cores(theirs, mp_count)
    kept, squares, *pieces = add_pair(here, kept, theirs, squares)
    pieces = [shift_chips(piece, step) for step, piece in enumerate(pieces, 1)]
    outgoing = route(target, kept, squares, *pieces)
    arrived = lax.all_to_all(outgoing, "rows", 0, 0, tiled=True)
    gram, routed = unpack(arrived)
    squares = arrived[:, capacity + 2 * docs : capacity + 2 * docs + 2, :docs]
    squares = jnp.sum(squares.astype(jnp.float32), axis=1)
    scale_rows = lax.rsqrt(squares / width + 1e-06).reshape(anchors, 1)

    grams = ring(gram, "mp", chips, mp_count, 2)
    grams = grams + [swap_cores(piece, mp_count) for piece in grams]
    slabs = lax.all_to_all(routed, "mp", 0, 0, tiled=True, axis_index_groups=by_y)
    slabs = [slabs, swap_cores(slabs, mp_count)]
    return solve(
        here, scale_rows, gain, state_all, *grams, *slabs
    )


def solution(mesh):
    return jax.shard_map(
        local,
        mesh=mesh,
        in_specs=(
            P("rows", None),
            P(),
            P(None, "mp"),
            P(None, "mp"),
            P(None, "mp"),
            P("mp", None),
            P(),
            P(),
            P("rows", None, "mp"),
            P("rows", None, "mp"),
            P("rows"),
            P(),
            P("rows", None),
            P("rows", "mp"),
            P("rows", None),
        ),
        out_specs=P("rows", "mp"),
        check_vma=False,
    )
```
